1024 devices in a mesh: lat: 32 (over x, z_hi, core), lon: 32 (over y, z_lo).
Axes of the slice: x: 4, y: 4, z: 32 (z_hi: 4, z_lo: 8; z = z_hi * 8 + z_lo), core: 2. Of those that a mesh axis runs over, the one named last changes fastest.
Arguments:
- grad_out: bfloat16 [704, 1440, 256], P('lat', 'lon'), may hold values from -6 to 6
- block_input: bfloat16 [704, 1440, 256], P('lat', 'lon'), may hold values from -6 to 6
- leg_table: bfloat16 [384, 384, 704], P('lat'), may hold values from -1 to 1, as said below
- spec_coeff: bfloat16 [384, 384, 2, 256], P(None, 'lat', None, 'lon'), may hold values from -6 to 6
- spec_filter: float32 [384, 256], P(None, 'lon'), may hold values from -6 to 6
- cycle_weight: float32 [704, 3], replicated, may hold values from 0.2 to 2
- cycle_shift: int32 [704, 3], replicated, may hold values from -1 to 1
- tap_weight: bfloat16 [3, 256, 256], replicated, may hold values from -0.21875 to 0.21875
Outputs:
- spec_grad: bfloat16 [384, 384, 2, 256], P(None, 'lat', None, 'lon')
- filter_grad: float32 [384, 256], P(None, 'lon')
- input_grad: bfloat16 [704, 1440, 256], P('lat', 'lon')
- taps_grad: float32 [3, 256, 256], replicated
The draws below stay inside these ranges and needn't reach their ends.
Inputs may be any that keep to these rules, and one draw needn't show every extreme that they name: `leg_table`: zero wherever the degree l is below the order m.
All inputs are finite; a program needn't handle non-finite values.
Results may differ from the reference program's by a relative error of at most 0.013.
Values may be sent and summed in bfloat16 or wider, within the bound.
No kernel may reach another device: no remote copies, remote signals or barrier semaphores. Data moves between devices by JAX's collectives and lax.ppermute only.
A program may use at most 64 MiB of HBM per device.

```python
import math
import jax
import jax.numpy as jnp
from jax import lax

NLAT = 704
NLON = 1440
C = 256
MMAX = 384
LMAX = 384
TAPS = 3
N_LAT = 32


def draw_leg_table(key, part):
    base = jnp.clip(jax.random.normal(key, (MMAX, LMAX, NLAT), jnp.float32), -6.0, 6.0)
    keep = (jnp.arange(LMAX)[None, :, None] >= jnp.arange(MMAX)[:, None, None]).astype(jnp.float32)
    return (base * keep / math.sqrt(NLAT)).astype(jnp.bfloat16)


def plant(drawn, key, low, largest):
    place = [jax.random.randint(jax.random.fold_in(key, axis), (), 0, length) for axis, length in enumerate(drawn.shape)]
    longest = drawn.shape.index(max(drawn.shape))
    next_to = place[:longest] + [(place[longest] + 1) % drawn.shape[longest]] + place[longest + 1:]
    return drawn.at[tuple(place)].set(low).at[tuple(next_to)].set(largest)


def level_of(key, dims, cuts, low, high):
    def one(position, parts):
        draws = jax.random.uniform(jax.random.fold_in(jax.random.fold_in(key, 6), position), (parts,), jnp.float32, low / len(cuts), high / len(cuts))
        return jnp.repeat(jnp.exp(draws), dims[position] // parts).reshape((-1,) + (1,) * (len(dims) - position - 1))

    gain = one(*cuts[0])
    for cut in cuts[1:]:
        gain = gain * one(*cut)
    return gain


def bell_draw(stream_key, extent, width, most, cuts=(), kind=jnp.bfloat16):
    gain = level_of(stream_key, extent, cuts, -0.22, 0.18) if cuts else 1.0
    array = jax.random.normal(stream_key, extent, jnp.float32) * width * gain
    return jnp.minimum(jnp.maximum(array, -most), most).astype(kind)


def setup_inputs(seed: int = 0) -> dict:
    streams_of = jax.random.split(jax.random.key(seed), 9)
    grad_out = bell_draw(streams_of[0], (NLAT, NLON, C), 1.0, 6.0, ((0, 32), (1, 32)))
    block_input = bell_draw(streams_of[1], (NLAT, NLON, C), 1.0, 6.0, ((0, 32), (1, 32)))
    leg_table = draw_leg_table(jax.random.fold_in(streams_of[8], 71), 0)
    spec_coeff = bell_draw(streams_of[3], (LMAX, MMAX, 2, C), 1.0, 6.0, ((1, 32), (3, 32)))
    spec_filter = bell_draw(streams_of[4], (LMAX, C), 1.0, 6.0, ((1, 32),), jnp.float32)
    cycle_weight = jnp.clip(jnp.exp(jax.random.uniform(streams_of[5], (NLAT, TAPS), jnp.float32, math.log(0.2), math.log(2.0))), 0.2, 2.0)
    cycle_shift = plant(jax.random.randint(streams_of[6], (NLAT, TAPS), -1, 2), jax.random.fold_in(streams_of[6], 1), -1, 1).astype(jnp.int32)
    tap_weight = bell_draw(streams_of[7], (TAPS, C, C), (TAPS * C) ** -0.5, 0.21875)
    return {"grad_out": grad_out, "block_input": block_input, "leg_table": leg_table, "spec_coeff": spec_coeff, "spec_filter": spec_filter, "cycle_weight": cycle_weight, "cycle_shift": cycle_shift, "tap_weight": tap_weight}


def fourier_table(lon_count, mode_count):
    longitude = jnp.arange(lon_count, dtype=jnp.int32)[:, None]
    orders = jnp.arange(mode_count, dtype=jnp.int32)[None, :]
    phase = (longitude * orders % lon_count).astype(jnp.float32) * (2.0 * math.pi / lon_count)
    table = jnp.stack([jnp.cos(phase), jnp.sin(phase)], axis=-1) / math.sqrt(lon_count)
    return table.astype(jnp.bfloat16)

def reference(grad_out, block_input, leg_table, spec_coeff, spec_filter, cycle_weight, cycle_shift, tap_weight):
    table = fourier_table(NLON, MMAX).reshape(NLON, 2 * MMAX)
    table_rows = table.T

    def analyse(cycle):
        return jnp.dot(table_rows, cycle, preferred_element_type=jnp.float32)
    fourier = lax.map(analyse, grad_out).astype(jnp.bfloat16)
    by_order = jnp.moveaxis(fourier.reshape(NLAT, MMAX, 2 * C), 1, 0)

    def project(pair):
        return jnp.dot(pair[0], pair[1], preferred_element_type=jnp.float32)
    degree = lax.map(project, (leg_table, by_order))
    degree = jnp.transpose(degree.reshape(MMAX, LMAX, 2, C), (1, 0, 2, 3))
    spec_grad = (degree * spec_filter[:, None, None, :]).astype(jnp.bfloat16)
    filter_grad = lax.optimization_barrier(jnp.sum(spec_coeff.astype(jnp.float32) * degree, axis=(1, 2))) / math.sqrt(2 * MMAX)
    band = NLAT // N_LAT
    grad_pad = jnp.pad(grad_out, ((1, 1), (0, 0), (0, 0)))
    weight_pad = jnp.pad(cycle_weight, ((1, 1), (0, 0)))
    shift_pad = jnp.pad(cycle_shift, ((1, 1), (0, 0)))

    def band_step(total, band_index):
        start = (band_index * band).astype(jnp.int32)
        inputs = lax.dynamic_slice_in_dim(block_input, start, band, 0).reshape(-1, C)
        result = jnp.zeros((band * NLON, C), jnp.float32)
        for tap_index, offset in enumerate((-1, 0, 1)):
            source = lax.dynamic_slice_in_dim(grad_pad, start + 1 - offset, band, 0)
            coef = lax.dynamic_slice_in_dim(weight_pad, start + 1 - offset, band, 0)[:, tap_index]
            shifts = lax.dynamic_slice_in_dim(shift_pad, start + 1 - offset, band, 0)[:, tap_index]
            picked = jnp.zeros((band, NLON, C), jnp.float32)
            for column_shift in (-1, 0, 1):
                rolled = jnp.roll(source, column_shift, axis=1).astype(jnp.float32)
                picked = picked + (shifts == column_shift).astype(jnp.float32)[:, None, None] * rolled
            spread = (coef[:, None, None] * picked).astype(jnp.bfloat16).reshape(-1, C)
            result = result + lax.dot_general(spread, tap_weight[tap_index], (((1,), (1,)), ((), ())), preferred_element_type=jnp.float32)
            total = total.at[tap_index].add(lax.dot_general(inputs, spread, (((0,), (0,)), ((), ())), preferred_element_type=jnp.float32))
        return (total, result.reshape(band, NLON, C).astype(jnp.bfloat16))
    start_total = jnp.zeros((TAPS, C, C), jnp.float32)
    total, bands = lax.scan(band_step, start_total, jnp.arange(N_LAT, dtype=jnp.int32))
    input_grad = bands.reshape(NLAT, NLON, C)
    taps_grad = total / math.sqrt(NLAT * NLON)
    return (spec_grad, filter_grad, input_grad, taps_grad)
```

```python
import functools
import math

import jax
import jax.numpy as jnp
import ml_dtypes
import numpy as np
from jax import lax
from jax.experimental import pallas as pl
from jax.experimental.pallas import tpu as pltpu
from jax.sharding import PartitionSpec as P

F32 = jnp.float32
BF16 = jnp.bfloat16
ROW = 8
LANES = 128


def ceil_to(value, step):
    return -(-value // step) * step


CORE = (1, 2)
Z_HI = (2, 4)
X = (8, 4)


def turn(total, digit, shift):
    stride, size = digit
    pairs = []
    for source in range(total):
        place = source // stride % size
        pairs.append((source, source + ((place + shift) % size - place) * stride))
    return pairs


def sum_over_digits(value, digits):
    total = lax.axis_size("lat")
    for digit in digits:
        parts = [value] + [
            lax.ppermute(value, "lat", turn(total, digit, shift)) for shift in range(1, digit[1])
        ]
        while len(parts) > 1:
            half = len(parts) // 2
            parts = [parts[i] + parts[i + half] for i in range(half)]
        value = parts[0]
    return value


def transform_constants(sectors, sector, orders, chans):
    lon_total = sectors * sector
    width = ceil_to(sector, 16)
    turns = orders // sectors
    p, j, q, t = (np.arange(n) for n in (sectors, sectors, sector, turns))
    across = 2 * np.pi * (p[:, None] * j[None, :] % sectors) / sectors
    eye = np.eye(chans)
    across = np.concatenate([np.kron(np.cos(across), eye), np.kron(np.sin(across), eye)])
    phase = 2 * np.pi * (p[:, None] * q[None, :]) / lon_total
    twiddle = np.zeros((2, sectors, ROW, width))
    twiddle[0, :, :, :sector] = (np.cos(phase) / math.sqrt(lon_total))[:, None]
    twiddle[1, :, :, :sector] = (np.sin(phase) / math.sqrt(lon_total))[:, None]
    twiddle = np.repeat(twiddle.reshape(2, sectors, ROW * width), chans, axis=1)
    within = 2 * np.pi * (t[:, None] * q[None, :] % sector) / sector
    c, s = np.cos(within), np.sin(within)
    inner = np.zeros((turns, 2, ROW, 2, ROW, width))
    for row in range(ROW):
        inner[:, 0, row, 0, row, :sector] = c
        inner[:, 0, row, 1, row, :sector] = -s
        inner[:, 1, row, 0, row, :sector] = s
        inner[:, 1, row, 1, row, :sector] = c
    inner = inner.reshape(turns * 2 * ROW, 2 * ROW * width)
    kind = ml_dtypes.bfloat16
    return across.astype(kind), twiddle.astype(np.float32), inner.astype(kind)


def turn_kernel(x_ref, o_ref, s_ref):
    rows, lons, _ = x_ref.shape
    s_ref[...] = jnp.zeros_like(s_ref)
    s_ref[:rows, :lons, :] = x_ref[...]
    o_ref[...] = s_ref[...].reshape(-1, s_ref.shape[2]).T


def channels_first(field):
    rows, lons, channels = field.shape
    tall, wide = ceil_to(rows, ROW), ceil_to(lons, 16)
    return pl.pallas_call(
        turn_kernel,
        out_shape=jax.ShapeDtypeStruct((channels, tall * wide), field.dtype),
        scratch_shapes=[pltpu.VMEM((tall, wide, channels), field.dtype)],
        compiler_params=pltpu.CompilerParams(vmem_limit_bytes=32 << 20),
        name="channels_first",
    )(field)


def fourier_kernel(blocks, turns, span, keep, r_ref, d_ref, tw_ref, w_ref, o_ref, g_ref):
    half = r_ref.shape[0]
    wide = tw_ref.shape[2]
    tall = blocks * ROW
    for block in range(blocks):
        field = r_ref[:, block * wide : (block + 1) * wide]
        a = jnp.dot(d_ref[:half], field, preferred_element_type=F32)
        b = jnp.dot(d_ref[half:], field, preferred_element_type=F32)
        re = (a * tw_ref[0] - b * tw_ref[1]).astype(BF16)
        im = (a * tw_ref[1] + b * tw_ref[0]).astype(BF16)
        nt = (((1,), (1,)), ((), ()))
        out = lax.dot_general(w_ref[:, :wide], re, nt, preferred_element_type=F32)
        out += lax.dot_general(w_ref[:, wide:], im, nt, preferred_element_type=F32)
        for t in range(turns):
            for r in range(2):
                g_ref[
                    r * tall + block * ROW : r * tall + (block + 1) * ROW,
                    t * half : (t + 1) * half,
                ] = out[(t * 2 + r) * ROW : (t * 2 + r + 1) * ROW]
    count = o_ref.shape[0]
    group = math.lcm(span, LANES)
    lane = lax.broadcasted_iota(jnp.int32, (keep, LANES), 1)
    rest = LANES - span
    for start in range(0, count * span, group):
        values = g_ref[:, start : start + group]
        for k in range(group // span):
            shift = (group - k * span) % group
            piece = pltpu.roll(values, shift, 1) if shift else values
            piece = piece[:, :LANES]
            tail = piece[keep:]
            folds = [pltpu.roll(tail, span - n * rest, 1) for n in range(span // rest)]
            folds.append(jnp.zeros((keep - len(folds) * tail.shape[0], LANES), F32))
            folded = jnp.concatenate(folds, axis=0)
            o_ref[start // span + k] = jnp.where(lane < span, piece[:keep], folded).astype(BF16)


def fold_sizes(rows, span):
    tall = 2 * ceil_to(rows, ROW)
    return tall, tall - ROW


def fourier_chunks(received, rows, sector, orders, groups):
    sectors, chans, lanes = received.shape
    blocks = ceil_to(rows, ROW) // ROW
    turns = orders // sectors
    span = orders // groups * chans
    tall, keep = fold_sizes(rows, span)
    across, twiddle, inner = transform_constants(sectors, sector, orders, chans)
    return pl.pallas_call(
        functools.partial(fourier_kernel, blocks, turns, span, keep),
        out_shape=jax.ShapeDtypeStruct((groups, keep, LANES), BF16),
        scratch_shapes=[pltpu.VMEM((tall, orders * chans), F32)],
        compiler_params=pltpu.CompilerParams(vmem_limit_bytes=48 << 20),
        name="fourier_chunks",
    )(
        received.reshape(sectors * chans, lanes),
        jnp.asarray(across),
        jnp.asarray(twiddle),
        jnp.asarray(inner),
    )


def unfold_kernel(rows, span, q_ref, o_ref, s_ref):
    count, keep, _ = q_ref.shape
    tall = ceil_to(rows, ROW)
    rest = LANES - span
    lane = lax.broadcasted_iota(jnp.int32, (ROW, LANES), 1)
    used = count * rows
    if s_ref.shape[0] > used:
        s_ref[used:, :] = jnp.zeros((s_ref.shape[0] - used, s_ref.shape[1]), F32)
    for n in range(count):
        block = q_ref[n].astype(F32)
        tail = pltpu.roll(block[:ROW], rest, 1)
        for k in range(1, span // rest):
            piece = pltpu.roll(block[k * ROW : (k + 1) * ROW], (k + 1) * rest, 1)
            tail = jnp.where(lane < k * rest, tail, piece)
        s_ref[n * rows : (n + 1) * rows, :LANES] = block[:rows]
        middle = keep - tall
        s_ref[n * rows : n * rows + middle, LANES:] = block[tall:keep]
        s_ref[n * rows + middle : (n + 1) * rows, LANES:] = tail[: rows - middle]
    orders, both, _ = o_ref.shape
    chans = both // 2
    for r in range(2):
        flipped = s_ref[:, r * LANES : (r + 1) * LANES].T[:, :used].astype(BF16)
        for m in range(orders):
            o_ref[m, r * chans : (r + 1) * chans, :] = flipped[m * chans : (m + 1) * chans]


def unfold(received, rows, orders, chans):
    count = received.shape[0]
    used = count * rows
    return pl.pallas_call(
        functools.partial(unfold_kernel, rows, orders * chans),
        out_shape=jax.ShapeDtypeStruct((orders, 2 * chans, used), BF16),
        scratch_shapes=[pltpu.VMEM((ceil_to(used, LANES), 2 * LANES), F32)],
        compiler_params=pltpu.CompilerParams(vmem_limit_bytes=32 << 20),
        name="unfold",
    )(received)


def padded_2(shard):
    for axis, dim in (("lat", 0), ("lon", 1)):
        size, length = (lax.axis_size(axis), shard.shape[dim])
        up = [(i, (i + 1) % size) for i in range(size)]
        down = [(j, i) for i, j in up]
        last = lax.index_in_dim(shard, length - 1, axis=dim, keepdims=False)
        first = lax.index_in_dim(shard, 0, axis=dim, keepdims=False)
        before = jnp.expand_dims(lax.ppermute(last, axis, up), dim)
        after = jnp.expand_dims(lax.ppermute(first, axis, down), dim)
        shard = jnp.concatenate([before, shard, after], axis=dim)
    return shard


def total_taps(part):
    shape = part.shape
    lat, lon = lax.axis_size("lat"), lax.axis_size("lon")
    core = lax.axis_index("lat") % 2
    swap = turn(lat, CORE, 1)
    halves = part.reshape(2, -1, shape[-1])
    mine = lax.dynamic_index_in_dim(halves, core, 0, keepdims=False)
    other = lax.dynamic_index_in_dim(halves, 1 - core, 0, keepdims=False)
    mine = mine + lax.ppermute(other, "lat", swap)
    rows, columns = mine.shape
    parts = columns // LANES
    high = rows * parts // lon
    chunks = mine.reshape(lon // parts, high, parts, LANES).transpose(0, 2, 1, 3)
    chunks = lax.all_to_all(chunks.reshape(lon, high, LANES), "lon", 0, 0)
    chunk = sum_over_digits(jnp.sum(chunks, axis=0), (X, Z_HI)).astype(BF16)
    chunks = lax.all_to_all(jnp.broadcast_to(chunk, (lon, high, LANES)), "lon", 0, 0)
    mine = chunks.reshape(lon // parts, parts, high, LANES).transpose(0, 2, 1, 3)
    mine = mine.reshape(rows, columns)
    other = lax.ppermute(mine, "lat", swap)
    low = jnp.where(core == 0, mine, other)
    high = jnp.where(core == 0, other, mine)
    return jnp.stack([low, high]).astype(F32).reshape(shape)


def disco(grad_out, block_input, cycle_weight, cycle_shift, tap_weight):
    rows_here, lons_here, channels = grad_out.shape
    lon_total = lons_here * lax.axis_size("lon")
    cycle_total = rows_here * lax.axis_size("lat")
    padded = padded_2(grad_out)
    cycle_start = lax.axis_index("lat") * rows_here
    weight_pad = jnp.pad(cycle_weight, ((1, 1), (0, 0)))
    shift_pad = jnp.pad(cycle_shift, ((1, 1), (0, 0)))
    flat_input = block_input.reshape(-1, channels)
    local_grad = jnp.zeros((rows_here * lons_here, channels), F32)
    partials = []
    for tap_index, offset in enumerate((-1, 0, 1)):
        source = padded[1 - offset : 1 - offset + rows_here]
        coef = lax.dynamic_slice_in_dim(weight_pad, cycle_start + 1 - offset, rows_here, 0)[
            :, tap_index
        ]
        shifts = lax.dynamic_slice_in_dim(shift_pad, cycle_start + 1 - offset, rows_here, 0)[
            :, tap_index
        ]
        picked = jnp.zeros((rows_here, lons_here, channels), F32)
        for column_shift in (-1, 0, 1):
            window = source[:, 1 - column_shift : 1 - column_shift + lons_here].astype(F32)
            picked = picked + (shifts == column_shift).astype(F32)[:, None, None] * window
        spread = (coef[:, None, None] * picked).astype(BF16).reshape(-1, channels)
        local_grad = local_grad + lax.dot_general(
            spread,
            tap_weight[tap_index],
            (((1,), (1,)), ((), ())),
            preferred_element_type=F32,
        )
        partials.append(
            lax.dot_general(flat_input, spread, (((0,), (0,)), ((), ())), preferred_element_type=F32)
        )
    taps_part = jnp.stack(partials) / math.sqrt(cycle_total * lon_total)
    return local_grad.reshape(rows_here, lons_here, channels).astype(BF16), taps_part


def on_device(
    grad_out, block_input, leg_table, spec_coeff, spec_filter, cycle_weight, cycle_shift, tap_weight
):
    rows_here, lons_here, channels = grad_out.shape
    lat, lon = lax.axis_size("lat"), lax.axis_size("lon")
    chans = channels // lon
    orders_here, degrees, _ = leg_table.shape
    orders = orders_here * lat

    sent = channels_first(grad_out).reshape(lon, chans, -1)
    rows = lax.all_to_all(sent, "lon", 0, 0)

    input_grad, taps_part = disco(grad_out, block_input, cycle_weight, cycle_shift, tap_weight)
    taps_grad = total_taps(taps_part)

    blocks = fourier_chunks(rows, rows_here, lons_here, orders, lat)
    columns = lax.all_to_all(blocks, "lat", 0, 0)
    fourier = unfold(columns, rows_here, orders_here, chans)
    degree = jnp.einsum("mla,mxa->mxl", leg_table, fourier, preferred_element_type=F32)
    degree = degree.reshape(orders_here, 2, chans, degrees)
    spec_grad = (degree * spec_filter.T).astype(BF16).transpose(3, 0, 1, 2)
    coeff = spec_coeff.transpose(1, 2, 3, 0).astype(F32)
    filter_part = jnp.sum(coeff * degree, axis=(0, 1)) / math.sqrt(2 * orders)
    filter_grad = sum_over_digits(filter_part, (CORE, X, Z_HI)).T
    return (spec_grad, filter_grad, input_grad, taps_grad)


def solution(mesh):
    in_specs = (
        P("lat", "lon", None),
        P("lat", "lon", None),
        P("lat", None, None),
        P(None, "lat", None, "lon"),
        P(None, "lon"),
        P(),
        P(),
        P(),
    )
    out_specs = (P(None, "lat", None, "lon"), P(None, "lon"), P("lat", "lon", None), P())
    return jax.shard_map(
        on_device, mesh=mesh, in_specs=in_specs, out_specs=out_specs, check_vma=False
    )
```

```python
import functools
import math

import jax
import jax.numpy as jnp
import ml_dtypes
import numpy as np
from jax import lax
from jax.experimental import pallas as pl
from jax.experimental.pallas import tpu as pltpu
from jax.sharding import PartitionSpec as P

F32 = jnp.float32
BF16 = jnp.bfloat16
ROW = 8
LANES = 128


def ceil_to(value, step):
    return -(-value // step) * step


PARTS = (("x", 4), ("z_hi", 4), ("core", 2))
LAT = tuple(name for name, _ in PARTS)
LON_BITS = (8, 16, 1, 2, 4)


def ring(size, step):
    return [(i, (i + step) % size) for i in range(size)]


def to_all(value, axes):
    count = lax.axis_size(axes)
    return lax.all_to_all(jnp.broadcast_to(value, (count, *value.shape)), axes, 0, 0)


def sum_over(value, stages):
    for axes in stages:
        value = jnp.sum(to_all(value, axes), axis=0)
    return value


def pairs(size, bit):
    return [(i, i ^ bit) for i in range(size)]


def scatter_rows(value, axis, bits):
    size, place = lax.axis_size(axis), lax.axis_index(axis)
    left = sorted(bits, reverse=True)
    value = value.reshape(*(2 for _ in left), -1, value.shape[-1])
    for step, bit in enumerate(bits):
        where = left.index(bit)
        left.remove(bit)
        low = lax.index_in_dim(value, 0, where, keepdims=False)
        high = lax.index_in_dim(value, 1, where, keepdims=False)
        upper = (place & bit) != 0
        value, sent = jnp.where(upper, high, low), jnp.where(upper, low, high)
        if step < 2:
            sent = sent.astype(BF16)
        value = value + lax.ppermute(sent, axis, pairs(size, bit)).astype(F32)
    return value


def sum_ring(value, axis):
    far, near, back = (lax.ppermute(value, axis, ring(4, step)) for step in (2, 1, 3))
    return (value + far) + (near + back)


def sum_doubling(value, axis):
    size, bit = lax.axis_size(axis), 1
    while bit < size:
        value = value + lax.ppermute(value, axis, pairs(size, bit))
        bit *= 2
    return value


def transform_constants(sectors, sector, orders, chans):
    lon_total = sectors * sector
    width = ceil_to(sector, 16)
    turns = orders // sectors
    p, j, q, t = (np.arange(n) for n in (sectors, sectors, sector, turns))
    across = 2 * np.pi * (p[:, None] * j[None, :] % sectors) / sectors
    eye = np.eye(chans)
    across = np.concatenate([np.kron(np.cos(across), eye), np.kron(np.sin(across), eye)])
    phase = 2 * np.pi * (p[:, None] * q[None, :]) / lon_total
    twiddle = np.zeros((2, sectors, ROW, width))
    twiddle[0, :, :, :sector] = (np.cos(phase) / math.sqrt(lon_total))[:, None]
    twiddle[1, :, :, :sector] = (np.sin(phase) / math.sqrt(lon_total))[:, None]
    twiddle = np.repeat(twiddle.reshape(2, sectors, ROW * width), chans, axis=1)
    within = 2 * np.pi * (t[:, None] * q[None, :] % sector) / sector
    c, s = np.cos(within), np.sin(within)
    inner = np.zeros((turns, 2, ROW, 2, ROW, width))
    for row in range(ROW):
        inner[:, 0, row, 0, row, :sector] = c
        inner[:, 0, row, 1, row, :sector] = -s
        inner[:, 1, row, 0, row, :sector] = s
        inner[:, 1, row, 1, row, :sector] = c
    inner = inner.reshape(turns * 2 * ROW, 2 * ROW * width)
    kind = ml_dtypes.bfloat16
    return across.astype(kind), twiddle.astype(np.float32), inner.astype(kind)


def turn_kernel(x_ref, o_ref, s_ref):
    rows, lons, _ = x_ref.shape
    s_ref[...] = jnp.zeros_like(s_ref)
    s_ref[:rows, :lons, :] = x_ref[...]
    o_ref[...] = s_ref[...].reshape(-1, s_ref.shape[2]).T


def channels_first(field):
    rows, lons, channels = field.shape
    tall, wide = ceil_to(rows, ROW), ceil_to(lons, 16)
    return pl.pallas_call(
        turn_kernel,
        out_shape=jax.ShapeDtypeStruct((channels, tall * wide), field.dtype),
        scratch_shapes=[pltpu.VMEM((tall, wide, channels), field.dtype)],
        compiler_params=pltpu.CompilerParams(vmem_limit_bytes=32 << 20),
        cost_estimate=pl.CostEstimate(
            flops=0, transcendentals=0, bytes_accessed=4 * channels * tall * wide
        ),
        name="channels_first",
    )(field)


def fourier_kernel(blocks, turns, span, keep, r_ref, d_ref, tw_ref, w_ref, o_ref, g_ref):
    half = r_ref.shape[0]
    wide = tw_ref.shape[2]
    tall = blocks * ROW
    for block in range(blocks):
        field = r_ref[:, block * wide : (block + 1) * wide]
        a = jnp.dot(d_ref[:half], field, preferred_element_type=F32)
        b = jnp.dot(d_ref[half:], field, preferred_element_type=F32)
        re = (a * tw_ref[0] - b * tw_ref[1]).astype(BF16)
        im = (a * tw_ref[1] + b * tw_ref[0]).astype(BF16)
        nt = (((1,), (1,)), ((), ()))
        out = lax.dot_general(w_ref[:, :wide], re, nt, preferred_element_type=F32)
        out += lax.dot_general(w_ref[:, wide:], im, nt, preferred_element_type=F32)
        for t in range(turns):
            for r in range(2):
                g_ref[
                    r * tall + block * ROW : r * tall + (block + 1) * ROW,
                    t * half : (t + 1) * half,
                ] = out[(t * 2 + r) * ROW : (t * 2 + r + 1) * ROW]
    count = o_ref.shape[0]
    group = math.lcm(span, LANES)
    lane = lax.broadcasted_iota(jnp.int32, (keep, LANES), 1)
    rest = LANES - span
    for start in range(0, count * span, group):
        values = g_ref[:, start : start + group]
        for k in range(group // span):
            shift = (group - k * span) % group
            piece = pltpu.roll(values, shift, 1) if shift else values
            piece = piece[:, :LANES]
            tail = piece[keep:]
            folds = [pltpu.roll(tail, span - n * rest, 1) for n in range(span // rest)]
            folds.append(jnp.zeros((keep - len(folds) * tail.shape[0], LANES), F32))
            folded = jnp.concatenate(folds, axis=0)
            o_ref[start // span + k] = jnp.where(lane < span, piece[:keep], folded).astype(BF16)


def fold_sizes(rows, span):
    tall = 2 * ceil_to(rows, ROW)
    return tall, tall - ROW


def fourier_chunks(received, rows, sector, orders, groups):
    sectors, chans, lanes = received.shape
    blocks = ceil_to(rows, ROW) // ROW
    turns = orders // sectors
    span = orders // groups * chans
    tall, keep = fold_sizes(rows, span)
    across, twiddle, inner = transform_constants(sectors, sector, orders, chans)
    return pl.pallas_call(
        functools.partial(fourier_kernel, blocks, turns, span, keep),
        out_shape=jax.ShapeDtypeStruct((groups, keep, LANES), BF16),
        scratch_shapes=[pltpu.VMEM((tall, orders * chans), F32)],
        compiler_params=pltpu.CompilerParams(vmem_limit_bytes=48 << 20),
        cost_estimate=pl.CostEstimate(
            flops=2 * sectors * chans * lanes * (2 * sectors * chans + 2 * turns * ROW * 2),
            transcendentals=0,
            bytes_accessed=2 * received.size + 2 * groups * keep * LANES + 4 * twiddle.size,
        ),
        name="fourier_chunks",
    )(
        received.reshape(sectors * chans, lanes),
        jnp.asarray(across),
        jnp.asarray(twiddle),
        jnp.asarray(inner),
    )


def unfold_kernel(rows, span, q_ref, o_ref, s_ref):
    count, keep, _ = q_ref.shape
    tall = ceil_to(rows, ROW)
    rest = LANES - span
    lane = lax.broadcasted_iota(jnp.int32, (ROW, LANES), 1)
    used = count * rows
    if s_ref.shape[0] > used:
        s_ref[used:, :] = jnp.zeros((s_ref.shape[0] - used, s_ref.shape[1]), F32)
    for n in range(count):
        block = q_ref[n].astype(F32)
        tail = pltpu.roll(block[:ROW], rest, 1)
        for k in range(1, span // rest):
            piece = pltpu.roll(block[k * ROW : (k + 1) * ROW], (k + 1) * rest, 1)
            tail = jnp.where(lane < k * rest, tail, piece)
        s_ref[n * rows : (n + 1) * rows, :LANES] = block[:rows]
        middle = keep - tall
        s_ref[n * rows : n * rows + middle, LANES:] = block[tall:keep]
        s_ref[n * rows + middle : (n + 1) * rows, LANES:] = tail[: rows - middle]
    orders, both, _ = o_ref.shape
    chans = both // 2
    for r in range(2):
        flipped = s_ref[:, r * LANES : (r + 1) * LANES].T[:, :used].astype(BF16)
        for m in range(orders):
            o_ref[m, r * chans : (r + 1) * chans, :] = flipped[m * chans : (m + 1) * chans]


def unfold(received, rows, orders, chans):
    count = received.shape[0]
    used = count * rows
    return pl.pallas_call(
        functools.partial(unfold_kernel, rows, orders * chans),
        out_shape=jax.ShapeDtypeStruct((orders, 2 * chans, used), BF16),
        scratch_shapes=[pltpu.VMEM((ceil_to(used, LANES), 2 * LANES), F32)],
        compiler_params=pltpu.CompilerParams(vmem_limit_bytes=32 << 20),
        cost_estimate=pl.CostEstimate(
            flops=0, transcendentals=0, bytes_accessed=2 * received.size + 4 * orders * chans * used
        ),
        name="unfold",
    )(received)


def select(shifts, windows):
    picked = jnp.zeros_like(windows[0])
    for shift, window in zip((-1, 0, 1), windows):
        picked = jnp.where((shifts == shift)[:, None, None], window, picked)
    return picked


def tap_rows(cycle_weight, cycle_shift, rows):
    start = lax.axis_index(LAT) * rows
    weights = jnp.pad(cycle_weight, ((1, 1), (0, 0)))
    shifts = jnp.pad(cycle_shift, ((1, 1), (0, 0)))
    taps = []
    for index, offset in enumerate((-1, 0, 1)):
        weight = lax.dynamic_slice_in_dim(weights, start + 1 - offset, rows, 0)[:, index]
        shift = lax.dynamic_slice_in_dim(shifts, start + 1 - offset, rows, 0)[:, index]
        taps.append((1 - offset, weight, shift))
    return taps


def scaled(weight, field):
    return (weight[:, None, None] * field.astype(F32)).astype(BF16)


def taps_part(grad_rows, block_input, before, after, taps):
    rows, lons, channels = block_input.shape
    wide = jnp.concatenate([before[:, None], block_input, after[:, None]], axis=1)
    partials = []
    for first, weight, shift in taps:
        spread = scaled(weight, grad_rows[first : first + rows])
        picked = select(shift, [wide[:, 1 + k : 1 + k + lons] for k in (-1, 0, 1)])
        partials.append(
            lax.dot_general(
                picked.reshape(-1, channels),
                spread.reshape(-1, channels),
                (((0,), (0,)), ((), ())),
                preferred_element_type=F32,
            )
        )
    return jnp.concatenate(partials, axis=0)


def input_part(grad_rows, before, after, taps, tap_weight):
    rows, lons, channels = grad_rows.shape
    rows -= 2
    wide = jnp.concatenate([before[:, None], grad_rows, after[:, None]], axis=1)
    total = jnp.zeros((rows * lons, channels), F32)
    for index, (first, weight, shift) in enumerate(taps):
        source = wide[first : first + rows]
        picked = select(shift, [source[:, 1 - k : 1 - k + lons] for k in (-1, 0, 1)])
        total = total + lax.dot_general(
            scaled(weight, picked).reshape(-1, channels),
            tap_weight[index],
            (((1,), (1,)), ((), ())),
            preferred_element_type=F32,
        )
    return total.reshape(rows, lons, channels).astype(BF16)


def on_device(
    grad_out, block_input, leg_table, spec_coeff, spec_filter, cycle_weight, cycle_shift, tap_weight
):
    rows_here, lons_here, channels = grad_out.shape
    lat, lon = lax.axis_size(LAT), lax.axis_size("lon")
    chans = channels // lon
    orders_here, degrees, _ = leg_table.shape
    orders = orders_here * lat
    core = lax.axis_index("core")
    swap = ring(2, 1)

    sent = channels_first(grad_out).reshape(lon, chans, -1)
    rows = lax.all_to_all(sent, "lon", 0, 0)

    above = lax.ppermute(grad_out[-1], LAT, ring(lat, 1))
    below = lax.ppermute(grad_out[0], LAT, ring(lat, -1))
    before = lax.ppermute(block_input[:, -1], "lon", ring(lon, 1))
    after = lax.ppermute(block_input[:, 0], "lon", ring(lon, -1))
    grad_rows = jnp.concatenate([above[None], grad_out, below[None]], axis=0)
    taps = tap_rows(cycle_weight, cycle_shift, rows_here)
    part = taps_part(grad_rows, block_input, before, after, taps)
    part = part / math.sqrt(rows_here * lat * lons_here * lon)

    left, right = part[:, : channels // 2], part[:, channels // 2 :]
    mine, other = jnp.where(core == 0, left, right), jnp.where(core == 0, right, left)
    high, width = mine.shape[0] // lon, mine.shape[1]
    rows, other = lax.optimization_barrier((rows, other))
    mine = mine + lax.ppermute(other, "core", swap)

    blocks = fourier_chunks(rows, rows_here, lons_here, orders, lat)
    blocks, edges = lax.optimization_barrier((blocks, (grad_rows[:, -1], grad_rows[:, 0])))
    columns = lax.all_to_all(blocks, LAT, 0, 0)

    before = lax.ppermute(edges[0], "lon", ring(lon, 1))
    after = lax.ppermute(edges[1], "lon", ring(lon, -1))
    input_grad = input_part(grad_rows, before, after, taps, tap_weight)

    chunk = scatter_rows(mine, "lon", LON_BITS)
    chunk = sum_ring(sum_doubling(chunk, "x"), "z_hi").astype(BF16)
    fourier = unfold(columns, rows_here, orders_here, chans)
    degree = jnp.einsum("mla,mxa->mxl", leg_table, fourier, preferred_element_type=F32)
    degree = degree.reshape(orders_here, 2, chans, degrees)
    spec_grad = (degree * spec_filter.T).astype(BF16).transpose(3, 0, 1, 2)
    coeff = spec_coeff.transpose(1, 2, 3, 0).astype(F32)
    filter_part = jnp.sum(coeff * degree, axis=(0, 1)) / math.sqrt(2 * orders)
    filter_part = sum_over(filter_part, (("x", "core"),))
    filter_part, chunk = lax.optimization_barrier((filter_part, chunk))
    filter_grad = sum_ring(filter_part, "z_hi").T

    mine = to_all(chunk, "lon").reshape(lon * high, width)
    mine, filter_grad = lax.optimization_barrier((mine, filter_grad))
    other = lax.ppermute(mine, "core", swap)
    left, right = jnp.where(core == 0, mine, other), jnp.where(core == 0, other, mine)
    taps_grad = jnp.concatenate([left, right], axis=1).astype(F32)
    taps_grad = taps_grad.reshape(len(taps), channels, channels)
    return (spec_grad, filter_grad, input_grad, taps_grad)


def solution(mesh):
    sizes = tuple(size for _, size in PARTS)
    split = jax.sharding.Mesh(mesh.devices.reshape(*sizes, mesh.shape["lon"]), (*LAT, "lon"))
    in_specs = (
        P(LAT, "lon", None),
        P(LAT, "lon", None),
        P(LAT, None, None),
        P(None, LAT, None, "lon"),
        P(None, "lon"),
        P(),
        P(),
        P(),
    )
    out_specs = (P(None, LAT, None, "lon"), P(None, "lon"), P(LAT, "lon", None), P())
    return jax.shard_map(
        on_device, mesh=split, in_specs=in_specs, out_specs=out_specs, check_vma=False
    )
```

```python
import functools
import math

import jax
import jax.numpy as jnp
import ml_dtypes
import numpy as np
from jax import lax
from jax.experimental import pallas as pl
from jax.experimental.pallas import tpu as pltpu
from jax.sharding import PartitionSpec as P

F32 = jnp.float32
BF16 = jnp.bfloat16
ROW = 8
LANES = 128


def ceil_to(value, step):
    return -(-value // step) * step


PARTS = (("x", 4), ("z_hi", 4), ("core", 2), ("y", 4), ("z_lo", 8))
LAT = ("x", "z_hi", "core")
LON = ("y", "z_lo")


def ring(size, step):
    return [(i, (i + step) % size) for i in range(size)]


def to_all(value, axes):
    count = lax.axis_size(axes)
    return lax.all_to_all(jnp.broadcast_to(value, (count, *value.shape)), axes, 0, 0)


def pairs(size, bit):
    return [(i, i ^ bit) for i in range(size)]


def scatter_rows(value, axis, bits):
    size, place = lax.axis_size(axis), lax.axis_index(axis)
    left = sorted(bits, reverse=True)
    value = value.reshape(*(2 for _ in left), -1, value.shape[-1])
    for bit in bits:
        where = left.index(bit)
        left.remove(bit)
        low = lax.index_in_dim(value, 0, where, keepdims=False)
        high = lax.index_in_dim(value, 1, where, keepdims=False)
        upper = (place & bit) != 0
        value, sent = jnp.where(upper, high, low), jnp.where(upper, low, high)
        value = value + lax.ppermute(sent.astype(BF16), axis, pairs(size, bit)).astype(F32)
    return value


def transform_constants(sectors, sector, orders, chans):
    lon_total = sectors * sector
    width = ceil_to(sector, 16)
    turns = orders // sectors
    p, j, q, t = (np.arange(n) for n in (sectors, sectors, sector, turns))
    across = 2 * np.pi * (p[:, None] * j[None, :] % sectors) / sectors
    eye = np.eye(chans)
    across = np.concatenate([np.kron(np.cos(across), eye), np.kron(np.sin(across), eye)])
    phase = 2 * np.pi * (p[:, None] * q[None, :]) / lon_total
    twiddle = np.zeros((2, sectors, ROW, width))
    twiddle[0, :, :, :sector] = (np.cos(phase) / math.sqrt(lon_total))[:, None]
    twiddle[1, :, :, :sector] = (np.sin(phase) / math.sqrt(lon_total))[:, None]
    twiddle = np.repeat(twiddle.reshape(2, sectors, ROW * width), chans, axis=1)
    within = 2 * np.pi * (t[:, None] * q[None, :] % sector) / sector
    c, s = np.cos(within), np.sin(within)
    inner = np.zeros((turns, 2, ROW, 2, ROW, width))
    for row in range(ROW):
        inner[:, 0, row, 0, row, :sector] = c
        inner[:, 0, row, 1, row, :sector] = -s
        inner[:, 1, row, 0, row, :sector] = s
        inner[:, 1, row, 1, row, :sector] = c
    inner = inner.reshape(turns * 2 * ROW, 2 * ROW * width)
    kind = ml_dtypes.bfloat16
    return across.astype(kind), twiddle.astype(np.float32), inner.astype(kind)


def turn_kernel(x_ref, o_ref, s_ref):
    rows, lons, _ = x_ref.shape
    s_ref[...] = jnp.zeros_like(s_ref)
    s_ref[:rows, :lons, :] = x_ref[...]
    o_ref[...] = s_ref[...].reshape(-1, s_ref.shape[2]).T


def channels_first(field):
    rows, lons, channels = field.shape
    tall, wide = ceil_to(rows, ROW), ceil_to(lons, 16)
    return pl.pallas_call(
        turn_kernel,
        out_shape=jax.ShapeDtypeStruct((channels, tall * wide), field.dtype),
        scratch_shapes=[pltpu.VMEM((tall, wide, channels), field.dtype)],
        compiler_params=pltpu.CompilerParams(vmem_limit_bytes=32 << 20),
        cost_estimate=pl.CostEstimate(
            flops=0, transcendentals=0, bytes_accessed=4 * channels * tall * wide
        ),
        name="channels_first",
    )(field)


def fourier_kernel(blocks, turns, span, keep, r_ref, d_ref, tw_ref, w_ref, o_ref, g_ref):
    half = r_ref.shape[0]
    wide = tw_ref.shape[2]
    tall = blocks * ROW
    for block in range(blocks):
        field = r_ref[:, block * wide : (block + 1) * wide]
        a = jnp.dot(d_ref[:half], field, preferred_element_type=F32)
        b = jnp.dot(d_ref[half:], field, preferred_element_type=F32)
        re = (a * tw_ref[0] - b * tw_ref[1]).astype(BF16)
        im = (a * tw_ref[1] + b * tw_ref[0]).astype(BF16)
        nt = (((1,), (1,)), ((), ()))
        out = lax.dot_general(w_ref[:, :wide], re, nt, preferred_element_type=F32)
        out += lax.dot_general(w_ref[:, wide:], im, nt, preferred_element_type=F32)
        for t in range(turns):
            for r in range(2):
                g_ref[
                    r * tall + block * ROW : r * tall + (block + 1) * ROW,
                    t * half : (t + 1) * half,
                ] = out[(t * 2 + r) * ROW : (t * 2 + r + 1) * ROW]
    count = o_ref.shape[0]
    group = math.lcm(span, LANES)
    lane = lax.broadcasted_iota(jnp.int32, (keep, LANES), 1)
    rest = LANES - span
    for start in range(0, count * span, group):
        values = g_ref[:, start : start + group]
        for k in range(group // span):
            shift = (group - k * span) % group
            piece = pltpu.roll(values, shift, 1) if shift else values
            piece = piece[:, :LANES]
            tail = piece[keep:]
            folds = [pltpu.roll(tail, span - n * rest, 1) for n in range(span // rest)]
            folds.append(jnp.zeros((keep - len(folds) * tail.shape[0], LANES), F32))
            folded = jnp.concatenate(folds, axis=0)
            o_ref[start // span + k] = jnp.where(lane < span, piece[:keep], folded).astype(BF16)


def fold_sizes(rows, span):
    tall = 2 * ceil_to(rows, ROW)
    return tall, tall - ROW


def fourier_chunks(received, rows, sector, orders, groups):
    sectors, chans, lanes = received.shape
    blocks = ceil_to(rows, ROW) // ROW
    turns = orders // sectors
    span = orders // groups * chans
    tall, keep = fold_sizes(rows, span)
    across, twiddle, inner = transform_constants(sectors, sector, orders, chans)
    return pl.pallas_call(
        functools.partial(fourier_kernel, blocks, turns, span, keep),
        out_shape=jax.ShapeDtypeStruct((groups, keep, LANES), BF16),
        scratch_shapes=[pltpu.VMEM((tall, orders * chans), F32)],
        compiler_params=pltpu.CompilerParams(vmem_limit_bytes=48 << 20),
        cost_estimate=pl.CostEstimate(
            flops=2 * sectors * chans * lanes * (2 * sectors * chans + 2 * turns * ROW * 2),
            transcendentals=0,
            bytes_accessed=2 * received.size + 2 * groups * keep * LANES + 4 * twiddle.size,
        ),
        name="fourier_chunks",
    )(
        received.reshape(sectors * chans, lanes),
        jnp.asarray(across),
        jnp.asarray(twiddle),
        jnp.asarray(inner),
    )


def unfold_kernel(rows, span, q_ref, o_ref, s_ref):
    count, keep, _ = q_ref.shape
    tall = ceil_to(rows, ROW)
    rest = LANES - span
    lane = lax.broadcasted_iota(jnp.int32, (ROW, LANES), 1)
    used = count * rows
    if s_ref.shape[0] > used:
        s_ref[used:, :] = jnp.zeros((s_ref.shape[0] - used, s_ref.shape[1]), F32)
    for n in range(count):
        block = q_ref[n].astype(F32)
        tail = pltpu.roll(block[:ROW], rest, 1)
        for k in range(1, span // rest):
            piece = pltpu.roll(block[k * ROW : (k + 1) * ROW], (k + 1) * rest, 1)
            tail = jnp.where(lane < k * rest, tail, piece)
        s_ref[n * rows : (n + 1) * rows, :LANES] = block[:rows]
        middle = keep - tall
        s_ref[n * rows : n * rows + middle, LANES:] = block[tall:keep]
        s_ref[n * rows + middle : (n + 1) * rows, LANES:] = tail[: rows - middle]
    orders, both, _ = o_ref.shape
    chans = both // 2
    for r in range(2):
        flipped = s_ref[:, r * LANES : (r + 1) * LANES].T[:, :used].astype(BF16)
        for m in range(orders):
            o_ref[m, r * chans : (r + 1) * chans, :] = flipped[m * chans : (m + 1) * chans]


def unfold(received, rows, orders, chans):
    count = received.shape[0]
    used = count * rows
    return pl.pallas_call(
        functools.partial(unfold_kernel, rows, orders * chans),
        out_shape=jax.ShapeDtypeStruct((orders, 2 * chans, used), BF16),
        scratch_shapes=[pltpu.VMEM((ceil_to(used, LANES), 2 * LANES), F32)],
        compiler_params=pltpu.CompilerParams(vmem_limit_bytes=32 << 20),
        cost_estimate=pl.CostEstimate(
            flops=0, transcendentals=0, bytes_accessed=2 * received.size + 4 * orders * chans * used
        ),
        name="unfold",
    )(received)


def select(shifts, windows):
    picked = jnp.zeros_like(windows[0])
    for shift, window in zip((-1, 0, 1), windows):
        picked = jnp.where((shifts == shift)[:, None, None], window, picked)
    return picked


def tap_rows(cycle_weight, cycle_shift, rows):
    start = lax.axis_index(LAT) * rows
    weights = jnp.pad(cycle_weight, ((1, 1), (0, 0)))
    shifts = jnp.pad(cycle_shift, ((1, 1), (0, 0)))
    taps = []
    for index, offset in enumerate((-1, 0, 1)):
        weight = lax.dynamic_slice_in_dim(weights, start + 1 - offset, rows, 0)[:, index]
        shift = lax.dynamic_slice_in_dim(shifts, start + 1 - offset, rows, 0)[:, index]
        taps.append((1 - offset, weight, shift))
    return taps


def scaled(weight, field):
    return (weight[:, None, None] * field.astype(F32)).astype(BF16)


def taps_part(grad_rows, block_input, before, after, taps):
    rows, lons, channels = block_input.shape
    wide = jnp.concatenate([before[:, None], block_input, after[:, None]], axis=1)
    partials = []
    for first, weight, shift in taps:
        spread = scaled(weight, grad_rows[first : first + rows])
        picked = select(shift, [wide[:, 1 + k : 1 + k + lons] for k in (-1, 0, 1)])
        partials.append(
            lax.dot_general(
                picked.reshape(-1, channels),
                spread.reshape(-1, channels),
                (((0,), (0,)), ((), ())),
                preferred_element_type=F32,
            )
        )
    return jnp.concatenate(partials, axis=0)


def input_part(grad_rows, before, after, taps, tap_weight):
    rows, lons, channels = grad_rows.shape
    rows -= 2
    wide = jnp.concatenate([before[:, None], grad_rows, after[:, None]], axis=1)
    total = jnp.zeros((rows * lons, channels), F32)
    for index, (first, weight, shift) in enumerate(taps):
        source = wide[first : first + rows]
        picked = select(shift, [source[:, 1 - k : 1 - k + lons] for k in (-1, 0, 1)])
        total = total + lax.dot_general(
            scaled(weight, picked).reshape(-1, channels),
            tap_weight[index],
            (((1,), (1,)), ((), ())),
            preferred_element_type=F32,
        )
    return total.reshape(rows, lons, channels).astype(BF16)


def on_device(
    grad_out, block_input, leg_table, spec_coeff, spec_filter, cycle_weight, cycle_shift, tap_weight
):
    rows_here, lons_here, channels = grad_out.shape
    lat, lon = lax.axis_size(LAT), lax.axis_size(LON)
    chans = channels // lon
    orders_here, degrees, _ = leg_table.shape
    orders = orders_here * lat
    core = lax.axis_index("core")
    swap = ring(2, 1)

    sent = channels_first(grad_out).reshape(lon, chans, -1)
    rows = lax.all_to_all(sent, LON, 0, 0)

    halos = (
        lax.ppermute(grad_out[-1], LAT, ring(lat, 1)),
        lax.ppermute(grad_out[0], LAT, ring(lat, -1)),
        lax.ppermute(block_input[:, -1], LON, ring(lon, 1)),
        lax.ppermute(block_input[:, 0], LON, ring(lon, -1)),
    )
    blocks = fourier_chunks(rows, rows_here, lons_here, orders, lat)
    blocks, (above, below, before, after) = lax.optimization_barrier((blocks, halos))
    columns = lax.all_to_all(blocks, LAT, 0, 0)

    grad_rows = jnp.concatenate([above[None], grad_out, below[None]], axis=0)
    taps = tap_rows(cycle_weight, cycle_shift, rows_here)
    part = taps_part(grad_rows, block_input, before, after, taps)
    part = part / math.sqrt(rows_here * lat * lons_here * lon)

    left, right = part[:, : channels // 2], part[:, channels // 2 :]
    mine, other = jnp.where(core == 0, left, right), jnp.where(core == 0, right, left)
    mine = mine + lax.ppermute(other, "core", swap)
    mine = scatter_rows(mine, "y", (1, 2)).astype(BF16)
    columns, mine = lax.optimization_barrier((columns, mine))
    ring_size = lax.axis_size("z_lo")
    chunk = lax.all_to_all(mine.reshape(ring_size, -1, mine.shape[1]), "z_lo", 0, 0)
    chunk = jnp.sum(chunk.astype(F32), axis=0)
    high, width = chunk.shape

    fourier = unfold(columns, rows_here, orders_here, chans)
    degree = jnp.einsum("mla,mxa->mxl", leg_table, fourier, preferred_element_type=F32)
    degree = degree.reshape(orders_here, 2, chans, degrees)
    spec_grad = (degree * spec_filter.T).astype(BF16).transpose(3, 0, 1, 2)
    coeff = spec_coeff.transpose(1, 2, 3, 0).astype(F32)
    filter_part = jnp.sum(coeff * degree, axis=(0, 1)) / math.sqrt(2 * orders)

    pieces = degrees // width
    both = [chunk] + [filter_part[:, i * width : (i + 1) * width] for i in range(pieces)]
    both = to_all(jnp.concatenate(both, axis=0), ("x", "core"))
    cores = jnp.sum(both.reshape(-1, 2, *both.shape[1:]), axis=0)
    chunk = jnp.where(core == 0, cores[0, :high], cores[1, :high])
    both = jnp.concatenate([chunk, cores[0, high:] + cores[1, high:]], axis=0)
    both, edges = lax.optimization_barrier((both, (grad_rows[:, -1], grad_rows[:, 0])))
    both = jnp.sum(to_all(both, "z_hi"), axis=0)
    filter_grad = both[high:].reshape(pieces, chans, width).transpose(0, 2, 1)
    filter_grad = filter_grad.reshape(degrees, chans)

    before = lax.ppermute(edges[0], LON, ring(lon, 1))
    after = lax.ppermute(edges[1], LON, ring(lon, -1))
    input_grad = input_part(grad_rows, before, after, taps, tap_weight)

    mine = to_all(both[:high].astype(BF16), "z_lo").reshape(-1, width)
    mine = to_all(mine, "y").reshape(-1, width)
    other = lax.ppermute(mine, "core", swap)
    left, right = jnp.where(core == 0, mine, other), jnp.where(core == 0, other, mine)
    taps_grad = jnp.concatenate([left, right], axis=1).astype(F32)
    taps_grad = taps_grad.reshape(len(taps), channels, channels)
    return (spec_grad, filter_grad, input_grad, taps_grad)


def solution(mesh):
    sizes = tuple(size for _, size in PARTS)
    names, sizes = zip(*PARTS)
    split = jax.sharding.Mesh(mesh.devices.reshape(sizes), names)
    in_specs = (
        P(LAT, LON, None),
        P(LAT, LON, None),
        P(LAT, None, None),
        P(None, LAT, None, LON),
        P(None, LON),
        P(),
        P(),
        P(),
    )
    out_specs = (P(None, LAT, None, LON), P(None, LON), P(LAT, LON, None), P())
    return jax.shard_map(
        on_device, mesh=split, in_specs=in_specs, out_specs=out_specs, check_vma=False
    )
```

```python
import functools
import math

import jax
import jax.numpy as jnp
import ml_dtypes
import numpy as np
from jax import lax
from jax.experimental import pallas as pl
from jax.experimental.pallas import tpu as pltpu
from jax.sharding import PartitionSpec as P

F32 = jnp.float32
BF16 = jnp.bfloat16
ROW = 8
LANES = 128


def ceil_to(value, step):
    return -(-value // step) * step


PARTS = (("x", 4), ("z_hi", 4), ("core", 2), ("y", 4), ("z_lo", 8))
LAT = ("x", "z_hi", "core")
LON = ("y", "z_lo")


def ring(size, step):
    return [(i, (i + step) % size) for i in range(size)]


def to_all(value, axes):
    count = lax.axis_size(axes)
    return lax.all_to_all(jnp.broadcast_to(value, (count, *value.shape)), axes, 0, 0)


def pairs(size, bit):
    return [(i, i ^ bit) for i in range(size)]


def scatter_rows(value, axis, bits):
    size, place = lax.axis_size(axis), lax.axis_index(axis)
    left = sorted(bits, reverse=True)
    value = value.reshape(*(2 for _ in left), -1, value.shape[-1])
    for bit in bits:
        where = left.index(bit)
        left.remove(bit)
        low = lax.index_in_dim(value, 0, where, keepdims=False)
        high = lax.index_in_dim(value, 1, where, keepdims=False)
        upper = (place & bit) != 0
        value, sent = jnp.where(upper, high, low), jnp.where(upper, low, high)
        value = value + lax.ppermute(sent.astype(BF16), axis, pairs(size, bit)).astype(F32)
    return value


def transform_constants(sectors, sector, orders, chans):
    lon_total = sectors * sector
    width = ceil_to(sector, 16)
    turns = orders // sectors
    p, j, q, t = (np.arange(n) for n in (sectors, sectors, sector, turns))
    across = 2 * np.pi * (p[:, None] * j[None, :] % sectors) / sectors
    eye = np.eye(chans)
    across = np.concatenate([np.kron(np.cos(across), eye), np.kron(np.sin(across), eye)])
    phase = 2 * np.pi * (p[:, None] * q[None, :]) / lon_total
    twiddle = np.zeros((2, sectors, ROW, width))
    twiddle[0, :, :, :sector] = (np.cos(phase) / math.sqrt(lon_total))[:, None]
    twiddle[1, :, :, :sector] = (np.sin(phase) / math.sqrt(lon_total))[:, None]
    twiddle = np.repeat(twiddle.reshape(2, sectors, ROW * width), chans, axis=1)
    within = 2 * np.pi * (t[:, None] * q[None, :] % sector) / sector
    c, s = np.cos(within), np.sin(within)
    inner = np.zeros((turns, 2, ROW, 2, ROW, width))
    for row in range(ROW):
        inner[:, 0, row, 0, row, :sector] = c
        inner[:, 0, row, 1, row, :sector] = -s
        inner[:, 1, row, 0, row, :sector] = s
        inner[:, 1, row, 1, row, :sector] = c
    inner = inner.reshape(turns * 2 * ROW, 2 * ROW * width)
    kind = ml_dtypes.bfloat16
    return across.astype(kind), twiddle.astype(np.float32), inner.astype(kind)


def turn_kernel(x_ref, o_ref, s_ref):
    rows, lons, _ = x_ref.shape
    s_ref[...] = jnp.zeros_like(s_ref)
    s_ref[:rows, :lons, :] = x_ref[...]
    o_ref[...] = s_ref[...].reshape(-1, s_ref.shape[2]).T


def channels_first(field):
    rows, lons, channels = field.shape
    tall, wide = ceil_to(rows, ROW), ceil_to(lons, 16)
    return pl.pallas_call(
        turn_kernel,
        out_shape=jax.ShapeDtypeStruct((channels, tall * wide), field.dtype),
        scratch_shapes=[pltpu.VMEM((tall, wide, channels), field.dtype)],
        compiler_params=pltpu.CompilerParams(vmem_limit_bytes=32 << 20),
        cost_estimate=pl.CostEstimate(
            flops=0, transcendentals=0, bytes_accessed=4 * channels * tall * wide
        ),
        name="channels_first",
    )(field)


def fourier_kernel(blocks, turns, span, keep, r_ref, d_ref, tw_ref, w_ref, o_ref, g_ref):
    half = r_ref.shape[0]
    wide = tw_ref.shape[2]
    tall = blocks * ROW
    for block in range(blocks):
        field = r_ref[:, block * wide : (block + 1) * wide]
        a = jnp.dot(d_ref[:half], field, preferred_element_type=F32)
        b = jnp.dot(d_ref[half:], field, preferred_element_type=F32)
        re = (a * tw_ref[0] - b * tw_ref[1]).astype(BF16)
        im = (a * tw_ref[1] + b * tw_ref[0]).astype(BF16)
        nt = (((1,), (1,)), ((), ()))
        out = lax.dot_general(w_ref[:, :wide], re, nt, preferred_element_type=F32)
        out += lax.dot_general(w_ref[:, wide:], im, nt, preferred_element_type=F32)
        for t in range(turns):
            for r in range(2):
                g_ref[
                    r * tall + block * ROW : r * tall + (block + 1) * ROW,
                    t * half : (t + 1) * half,
                ] = out[(t * 2 + r) * ROW : (t * 2 + r + 1) * ROW]
    count = o_ref.shape[0]
    group = math.lcm(span, LANES)
    lane = lax.broadcasted_iota(jnp.int32, (keep, LANES), 1)
    rest = LANES - span
    for start in range(0, count * span, group):
        values = g_ref[:, start : start + group]
        for k in range(group // span):
            shift = (group - k * span) % group
            piece = pltpu.roll(values, shift, 1) if shift else values
            piece = piece[:, :LANES]
            tail = piece[keep:]
            folds = [pltpu.roll(tail, span - n * rest, 1) for n in range(span // rest)]
            folds.append(jnp.zeros((keep - len(folds) * tail.shape[0], LANES), F32))
            folded = jnp.concatenate(folds, axis=0)
            o_ref[start // span + k] = jnp.where(lane < span, piece[:keep], folded).astype(BF16)


def fold_sizes(rows, span):
    tall = 2 * ceil_to(rows, ROW)
    return tall, tall - ROW


def fourier_chunks(received, rows, sector, orders, groups):
    sectors, chans, lanes = received.shape
    blocks = ceil_to(rows, ROW) // ROW
    turns = orders // sectors
    span = orders // groups * chans
    tall, keep = fold_sizes(rows, span)
    across, twiddle, inner = transform_constants(sectors, sector, orders, chans)
    return pl.pallas_call(
        functools.partial(fourier_kernel, blocks, turns, span, keep),
        out_shape=jax.ShapeDtypeStruct((groups, keep, LANES), BF16),
        scratch_shapes=[pltpu.VMEM((tall, orders * chans), F32)],
        compiler_params=pltpu.CompilerParams(vmem_limit_bytes=48 << 20),
        cost_estimate=pl.CostEstimate(
            flops=2 * sectors * chans * lanes * (2 * sectors * chans + 2 * turns * ROW * 2),
            transcendentals=0,
            bytes_accessed=2 * received.size + 2 * groups * keep * LANES + 4 * twiddle.size,
        ),
        name="fourier_chunks",
    )(
        received.reshape(sectors * chans, lanes),
        jnp.asarray(across),
        jnp.asarray(twiddle),
        jnp.asarray(inner),
    )


def unfold_kernel(rows, span, q_ref, o_ref, s_ref):
    count, keep, _ = q_ref.shape
    tall = ceil_to(rows, ROW)
    rest = LANES - span
    lane = lax.broadcasted_iota(jnp.int32, (ROW, LANES), 1)
    used = count * rows
    if s_ref.shape[0] > used:
        s_ref[used:, :] = jnp.zeros((s_ref.shape[0] - used, s_ref.shape[1]), F32)
    for n in range(count):
        block = q_ref[n].astype(F32)
        tail = pltpu.roll(block[:ROW], rest, 1)
        for k in range(1, span // rest):
            piece = pltpu.roll(block[k * ROW : (k + 1) * ROW], (k + 1) * rest, 1)
            tail = jnp.where(lane < k * rest, tail, piece)
        s_ref[n * rows : (n + 1) * rows, :LANES] = block[:rows]
        middle = keep - tall
        s_ref[n * rows : n * rows + middle, LANES:] = block[tall:keep]
        s_ref[n * rows + middle : (n + 1) * rows, LANES:] = tail[: rows - middle]
    orders, both, _ = o_ref.shape
    chans = both // 2
    for r in range(2):
        flipped = s_ref[:, r * LANES : (r + 1) * LANES].T[:, :used].astype(BF16)
        for m in range(orders):
            o_ref[m, r * chans : (r + 1) * chans, :] = flipped[m * chans : (m + 1) * chans]


def unfold(received, rows, orders, chans):
    count = received.shape[0]
    used = count * rows
    return pl.pallas_call(
        functools.partial(unfold_kernel, rows, orders * chans),
        out_shape=jax.ShapeDtypeStruct((orders, 2 * chans, used), BF16),
        scratch_shapes=[pltpu.VMEM((ceil_to(used, LANES), 2 * LANES), F32)],
        compiler_params=pltpu.CompilerParams(vmem_limit_bytes=32 << 20),
        cost_estimate=pl.CostEstimate(
            flops=0, transcendentals=0, bytes_accessed=2 * received.size + 4 * orders * chans * used
        ),
        name="unfold",
    )(received)


def select(shifts, windows):
    picked = jnp.zeros_like(windows[0])
    for shift, window in zip((-1, 0, 1), windows):
        picked = jnp.where((shifts == shift)[:, None, None], window, picked)
    return picked


def tap_rows(cycle_weight, cycle_shift, rows):
    start = lax.axis_index(LAT) * rows
    weights = jnp.pad(cycle_weight, ((1, 1), (0, 0)))
    shifts = jnp.pad(cycle_shift, ((1, 1), (0, 0)))
    taps = []
    for index, offset in enumerate((-1, 0, 1)):
        weight = lax.dynamic_slice_in_dim(weights, start + 1 - offset, rows, 0)[:, index]
        shift = lax.dynamic_slice_in_dim(shifts, start + 1 - offset, rows, 0)[:, index]
        taps.append((1 - offset, weight, shift))
    return taps


def scaled(weight, field):
    return (weight[:, None, None] * field.astype(F32)).astype(BF16)


def taps_part(grad_rows, block_input, before, after, taps):
    rows, lons, channels = block_input.shape
    wide = jnp.concatenate([before[:, None], block_input, after[:, None]], axis=1)
    partials = []
    for first, weight, shift in taps:
        spread = scaled(weight, grad_rows[first : first + rows])
        picked = select(shift, [wide[:, 1 + k : 1 + k + lons] for k in (-1, 0, 1)])
        partials.append(
            lax.dot_general(
                picked.reshape(-1, channels),
                spread.reshape(-1, channels),
                (((0,), (0,)), ((), ())),
                preferred_element_type=F32,
            )
        )
    return jnp.concatenate(partials, axis=0)


def input_part(grad_rows, before, after, taps, tap_weight):
    rows, lons, channels = grad_rows.shape
    rows -= 2
    wide = jnp.concatenate([before[:, None], grad_rows, after[:, None]], axis=1)
    total = jnp.zeros((rows * lons, channels), F32)
    for index, (first, weight, shift) in enumerate(taps):
        source = wide[first : first + rows]
        picked = select(shift, [source[:, 1 - k : 1 - k + lons] for k in (-1, 0, 1)])
        total = total + lax.dot_general(
            scaled(weight, picked).reshape(-1, channels),
            tap_weight[index],
            (((1,), (1,)), ((), ())),
            preferred_element_type=F32,
        )
    return total.reshape(rows, lons, channels).astype(BF16)


def on_device(
    grad_out, block_input, leg_table, spec_coeff, spec_filter, cycle_weight, cycle_shift, tap_weight
):
    rows_here, lons_here, channels = grad_out.shape
    lat, lon = lax.axis_size(LAT), lax.axis_size(LON)
    chans = channels // lon
    orders_here, degrees, _ = leg_table.shape
    orders = orders_here * lat
    core = lax.axis_index("core")
    swap = ring(2, 1)

    sent = channels_first(grad_out).reshape(lon, chans, -1)
    rows = lax.all_to_all(sent, LON, 0, 0)

    halos = (
        lax.ppermute(grad_out[-1], LAT, ring(lat, 1)),
        lax.ppermute(grad_out[0], LAT, ring(lat, -1)),
        lax.ppermute(block_input[:, -1], LON, ring(lon, 1)),
        lax.ppermute(block_input[:, 0], LON, ring(lon, -1)),
    )
    blocks = fourier_chunks(rows, rows_here, lons_here, orders, lat)
    blocks, (above, below, before, after) = lax.optimization_barrier((blocks, halos))
    columns = lax.all_to_all(blocks, LAT, 0, 0)

    grad_rows = jnp.concatenate([above[None], grad_out, below[None]], axis=0)
    taps = tap_rows(cycle_weight, cycle_shift, rows_here)
    part = taps_part(grad_rows, block_input, before, after, taps)
    part = part / math.sqrt(rows_here * lat * lons_here * lon)

    left, right = part[:, : channels // 2], part[:, channels // 2 :]
    mine, other = jnp.where(core == 0, left, right), jnp.where(core == 0, right, left)
    mine = mine + lax.ppermute(other, "core", swap)
    mine = scatter_rows(mine, "y", (1, 2)).astype(BF16)
    mine, edges = lax.optimization_barrier((mine, (grad_rows[:, -1], grad_rows[:, 0])))
    edges = (
        lax.ppermute(edges[0], LON, ring(lon, 1)),
        lax.ppermute(edges[1], LON, ring(lon, -1)),
    )
    columns, mine, (before, after) = lax.optimization_barrier((columns, mine, edges))
    ring_size = lax.axis_size("z_lo")
    chunk = lax.all_to_all(mine.reshape(ring_size, -1, mine.shape[1]), "z_lo", 0, 0)
    chunk = jnp.sum(chunk.astype(F32), axis=0)
    high, width = chunk.shape

    fourier = unfold(columns, rows_here, orders_here, chans)
    degree = jnp.einsum("mla,mxa->mxl", leg_table, fourier, preferred_element_type=F32)
    degree = degree.reshape(orders_here, 2, chans, degrees)
    spec_grad = (degree * spec_filter.T).astype(BF16).transpose(3, 0, 1, 2)
    coeff = spec_coeff.transpose(1, 2, 3, 0).astype(F32)
    filter_part = jnp.sum(coeff * degree, axis=(0, 1)) / math.sqrt(2 * orders)

    pieces = degrees // width
    both = [chunk] + [filter_part[:, i * width : (i + 1) * width] for i in range(pieces)]
    both = to_all(jnp.concatenate(both, axis=0).astype(BF16), ("x", "core")).astype(F32)
    cores = jnp.sum(both.reshape(-1, 2, *both.shape[1:]), axis=0)
    chunk = jnp.where(core == 0, cores[0, :high], cores[1, :high])
    both = jnp.concatenate([chunk, cores[0, high:] + cores[1, high:]], axis=0)
    both = jnp.sum(to_all(both.astype(BF16), "z_hi").astype(F32), axis=0)
    filter_grad = both[high:].reshape(pieces, chans, width).transpose(0, 2, 1)
    filter_grad = filter_grad.reshape(degrees, chans)

    input_grad = input_part(grad_rows, before, after, taps, tap_weight)

    mine = to_all(both[:high].astype(BF16), "z_lo").reshape(-1, width)
    mine = to_all(mine, ("core", "y")).reshape(2, -1, width)
    taps_grad = jnp.concatenate([mine[0], mine[1]], axis=1).astype(F32)
    taps_grad = taps_grad.reshape(len(taps), channels, channels)
    return (spec_grad, filter_grad, input_grad, taps_grad)


def solution(mesh):
    sizes = tuple(size for _, size in PARTS)
    names, sizes = zip(*PARTS)
    split = jax.sharding.Mesh(mesh.devices.reshape(sizes), names)
    in_specs = (
        P(LAT, LON, None),
        P(LAT, LON, None),
        P(LAT, None, None),
        P(None, LAT, None, LON),
        P(None, LON),
        P(),
        P(),
        P(),
    )
    out_specs = (P(None, LAT, None, LON), P(None, LON), P(LAT, LON, None), P())
    return jax.shard_map(
        on_device, mesh=split, in_specs=in_specs, out_specs=out_specs, check_vma=False
    )
```

```python
import functools
import math

import jax
import jax.numpy as jnp
import ml_dtypes
import numpy as np
from jax import lax
from jax.experimental import pallas as pl
from jax.experimental.pallas import tpu as pltpu
from jax.sharding import PartitionSpec as P

F32 = jnp.float32
BF16 = jnp.bfloat16
ROW = 8
LANES = 128


def ceil_to(value, step):
    return -(-value // step) * step


PARTS = (("x", 4), ("z_hi", 4), ("core", 2), ("y", 4), ("z_lo", 8))
LAT = ("x", "z_hi", "core")
LON = ("y", "z_lo")


def ring(size, step):
    return [(i, (i + step) % size) for i in range(size)]


def to_all(value, axes):
    count = lax.axis_size(axes)
    return lax.all_to_all(jnp.broadcast_to(value, (count, *value.shape)), axes, 0, 0)


def pairs(size, bit):
    return [(i, i ^ bit) for i in range(size)]


def halve(value, axis, bit, where):
    low = lax.index_in_dim(value, 0, where, keepdims=False)
    high = lax.index_in_dim(value, 1, where, keepdims=False)
    upper = (lax.axis_index(axis) & bit) != 0
    value, sent = jnp.where(upper, high, low), jnp.where(upper, low, high)
    received = lax.ppermute(sent.astype(BF16), axis, pairs(lax.axis_size(axis), bit))
    return value + received.astype(F32)


def transform_constants(sectors, sector, orders, chans):
    lon_total = sectors * sector
    width = ceil_to(sector, 16)
    turns = orders // sectors
    p, j, q, t = (np.arange(n) for n in (sectors, sectors, sector, turns))
    across = 2 * np.pi * (p[:, None] * j[None, :] % sectors) / sectors
    eye = np.eye(chans)
    across = np.concatenate([np.kron(np.cos(across), eye), np.kron(np.sin(across), eye)])
    phase = 2 * np.pi * (p[:, None] * q[None, :]) / lon_total
    twiddle = np.zeros((2, sectors, ROW, width))
    twiddle[0, :, :, :sector] = (np.cos(phase) / math.sqrt(lon_total))[:, None]
    twiddle[1, :, :, :sector] = (np.sin(phase) / math.sqrt(lon_total))[:, None]
    twiddle = np.repeat(twiddle.reshape(2, sectors, ROW * width), chans, axis=1)
    within = 2 * np.pi * (t[:, None] * q[None, :] % sector) / sector
    c, s = np.cos(within), np.sin(within)
    inner = np.zeros((turns, 2, ROW, 2, ROW, width))
    for row in range(ROW):
        inner[:, 0, row, 0, row, :sector] = c
        inner[:, 0, row, 1, row, :sector] = -s
        inner[:, 1, row, 0, row, :sector] = s
        inner[:, 1, row, 1, row, :sector] = c
    inner = inner.reshape(turns * 2 * ROW, 2 * ROW * width)
    kind = ml_dtypes.bfloat16
    return across.astype(kind), twiddle.astype(np.float32), inner.astype(kind)


def turn_kernel(x_ref, o_ref, s_ref):
    rows, lons, _ = x_ref.shape
    s_ref[...] = jnp.zeros_like(s_ref)
    s_ref[:rows, :lons, :] = x_ref[...]
    o_ref[...] = s_ref[...].reshape(-1, s_ref.shape[2]).T


def channels_first(field):
    rows, lons, channels = field.shape
    tall, wide = ceil_to(rows, ROW), ceil_to(lons, 16)
    return pl.pallas_call(
        turn_kernel,
        out_shape=jax.ShapeDtypeStruct((channels, tall * wide), field.dtype),
        scratch_shapes=[pltpu.VMEM((tall, wide, channels), field.dtype)],
        compiler_params=pltpu.CompilerParams(vmem_limit_bytes=32 << 20),
        cost_estimate=pl.CostEstimate(
            flops=0, transcendentals=0, bytes_accessed=4 * channels * tall * wide
        ),
        name="channels_first",
    )(field)


def fourier_kernel(blocks, turns, span, keep, r_ref, d_ref, tw_ref, w_ref, o_ref, g_ref):
    half = r_ref.shape[0]
    wide = tw_ref.shape[2]
    tall = blocks * ROW
    for block in range(blocks):
        field = r_ref[:, block * wide : (block + 1) * wide]
        a = jnp.dot(d_ref[:half], field, preferred_element_type=F32)
        b = jnp.dot(d_ref[half:], field, preferred_element_type=F32)
        re = (a * tw_ref[0] - b * tw_ref[1]).astype(BF16)
        im = (a * tw_ref[1] + b * tw_ref[0]).astype(BF16)
        nt = (((1,), (1,)), ((), ()))
        out = lax.dot_general(w_ref[:, :wide], re, nt, preferred_element_type=F32)
        out += lax.dot_general(w_ref[:, wide:], im, nt, preferred_element_type=F32)
        for t in range(turns):
            for r in range(2):
                g_ref[
                    r * tall + block * ROW : r * tall + (block + 1) * ROW,
                    t * half : (t + 1) * half,
                ] = out[(t * 2 + r) * ROW : (t * 2 + r + 1) * ROW]
    count = o_ref.shape[0]
    group = math.lcm(span, LANES)
    lane = lax.broadcasted_iota(jnp.int32, (keep, LANES), 1)
    rest = LANES - span
    for start in range(0, count * span, group):
        values = g_ref[:, start : start + group]
        for k in range(group // span):
            shift = (group - k * span) % group
            piece = pltpu.roll(values, shift, 1) if shift else values
            piece = piece[:, :LANES]
            tail = piece[keep:]
            folds = [pltpu.roll(tail, span - n * rest, 1) for n in range(span // rest)]
            folds.append(jnp.zeros((keep - len(folds) * tail.shape[0], LANES), F32))
            folded = jnp.concatenate(folds, axis=0)
            o_ref[start // span + k] = jnp.where(lane < span, piece[:keep], folded).astype(BF16)


def fold_sizes(rows, span):
    tall = 2 * ceil_to(rows, ROW)
    return tall, tall - ROW


def fourier_chunks(received, rows, sector, orders, groups):
    sectors, chans, lanes = received.shape
    blocks = ceil_to(rows, ROW) // ROW
    turns = orders // sectors
    span = orders // groups * chans
    tall, keep = fold_sizes(rows, span)
    across, twiddle, inner = transform_constants(sectors, sector, orders, chans)
    return pl.pallas_call(
        functools.partial(fourier_kernel, blocks, turns, span, keep),
        out_shape=jax.ShapeDtypeStruct((groups, keep, LANES), BF16),
        scratch_shapes=[pltpu.VMEM((tall, orders * chans), F32)],
        compiler_params=pltpu.CompilerParams(vmem_limit_bytes=48 << 20),
        cost_estimate=pl.CostEstimate(
            flops=2 * sectors * chans * lanes * (2 * sectors * chans + 2 * turns * ROW * 2),
            transcendentals=0,
            bytes_accessed=2 * received.size + 2 * groups * keep * LANES + 4 * twiddle.size,
        ),
        name="fourier_chunks",
    )(
        received.reshape(sectors * chans, lanes),
        jnp.asarray(across),
        jnp.asarray(twiddle),
        jnp.asarray(inner),
    )


def unfold_kernel(rows, span, q_ref, o_ref, s_ref):
    count, keep, _ = q_ref.shape
    tall = ceil_to(rows, ROW)
    rest = LANES - span
    lane = lax.broadcasted_iota(jnp.int32, (ROW, LANES), 1)
    used = count * rows
    if s_ref.shape[0] > used:
        s_ref[used:, :] = jnp.zeros((s_ref.shape[0] - used, s_ref.shape[1]), F32)
    for n in range(count):
        block = q_ref[n].astype(F32)
        tail = pltpu.roll(block[:ROW], rest, 1)
        for k in range(1, span // rest):
            piece = pltpu.roll(block[k * ROW : (k + 1) * ROW], (k + 1) * rest, 1)
            tail = jnp.where(lane < k * rest, tail, piece)
        s_ref[n * rows : (n + 1) * rows, :LANES] = block[:rows]
        middle = keep - tall
        s_ref[n * rows : n * rows + middle, LANES:] = block[tall:keep]
        s_ref[n * rows + middle : (n + 1) * rows, LANES:] = tail[: rows - middle]
    orders, both, _ = o_ref.shape
    chans = both // 2
    for r in range(2):
        flipped = s_ref[:, r * LANES : (r + 1) * LANES].T[:, :used].astype(BF16)
        for m in range(orders):
            o_ref[m, r * chans : (r + 1) * chans, :] = flipped[m * chans : (m + 1) * chans]


def unfold(received, rows, orders, chans):
    count = received.shape[0]
    used = count * rows
    return pl.pallas_call(
        functools.partial(unfold_kernel, rows, orders * chans),
        out_shape=jax.ShapeDtypeStruct((orders, 2 * chans, used), BF16),
        scratch_shapes=[pltpu.VMEM((ceil_to(used, LANES), 2 * LANES), F32)],
        compiler_params=pltpu.CompilerParams(vmem_limit_bytes=32 << 20),
        cost_estimate=pl.CostEstimate(
            flops=0, transcendentals=0, bytes_accessed=2 * received.size + 4 * orders * chans * used
        ),
        name="unfold",
    )(received)


def select(shifts, windows):
    picked = jnp.zeros_like(windows[0])
    for shift, window in zip((-1, 0, 1), windows):
        picked = jnp.where((shifts == shift)[:, None, None], window, picked)
    return picked


def tap_rows(cycle_weight, cycle_shift, rows):
    start = lax.axis_index(LAT) * rows
    weights = jnp.pad(cycle_weight, ((1, 1), (0, 0)))
    shifts = jnp.pad(cycle_shift, ((1, 1), (0, 0)))
    taps = []
    for index, offset in enumerate((-1, 0, 1)):
        weight = lax.dynamic_slice_in_dim(weights, start + 1 - offset, rows, 0)[:, index]
        shift = lax.dynamic_slice_in_dim(shifts, start + 1 - offset, rows, 0)[:, index]
        taps.append((1 - offset, weight, shift))
    return taps


def scaled(weight, field):
    return (weight[:, None, None] * field.astype(F32)).astype(BF16)


def taps_part(grad_rows, block_input, before, after, taps):
    rows, lons, channels = block_input.shape
    wide = jnp.concatenate([before[:, None], block_input, after[:, None]], axis=1)
    partials = []
    for first, weight, shift in taps:
        spread = scaled(weight, grad_rows[first : first + rows])
        picked = select(shift, [wide[:, 1 + k : 1 + k + lons] for k in (-1, 0, 1)])
        partials.append(
            lax.dot_general(
                picked.reshape(-1, channels),
                spread.reshape(-1, channels),
                (((0,), (0,)), ((), ())),
                preferred_element_type=F32,
            )
        )
    return jnp.concatenate(partials, axis=0)


def input_part(grad_rows, before, after, taps, tap_weight):
    rows, lons, channels = grad_rows.shape
    rows -= 2
    wide = jnp.concatenate([before[:, None], grad_rows, after[:, None]], axis=1)
    total = jnp.zeros((rows * lons, channels), F32)
    for index, (first, weight, shift) in enumerate(taps):
        source = wide[first : first + rows]
        picked = select(shift, [source[:, 1 - k : 1 - k + lons] for k in (-1, 0, 1)])
        total = total + lax.dot_general(
            scaled(weight, picked).reshape(-1, channels),
            tap_weight[index],
            (((1,), (1,)), ((), ())),
            preferred_element_type=F32,
        )
    return total.reshape(rows, lons, channels).astype(BF16)


def on_device(
    grad_out, block_input, leg_table, spec_coeff, spec_filter, cycle_weight, cycle_shift, tap_weight
):
    rows_here, lons_here, channels = grad_out.shape
    lat, lon = lax.axis_size(LAT), lax.axis_size(LON)
    chans = channels // lon
    orders_here, degrees, _ = leg_table.shape
    orders = orders_here * lat
    core = lax.axis_index("core")
    swap = ring(2, 1)

    sent = channels_first(grad_out).reshape(lon, chans, -1)
    rows = lax.all_to_all(sent, LON, 0, 0)

    halos = (
        lax.ppermute(grad_out[-1], LAT, ring(lat, 1)),
        lax.ppermute(grad_out[0], LAT, ring(lat, -1)),
        lax.ppermute(block_input[:, -1], LON, ring(lon, 1)),
        lax.ppermute(block_input[:, 0], LON, ring(lon, -1)),
    )
    blocks = fourier_chunks(rows, rows_here, lons_here, orders, lat)
    blocks, (above, below, before, after) = lax.optimization_barrier((blocks, halos))
    columns = lax.all_to_all(blocks, LAT, 0, 0)

    grad_rows = jnp.concatenate([above[None], grad_out, below[None]], axis=0)
    taps = tap_rows(cycle_weight, cycle_shift, rows_here)
    part = taps_part(grad_rows, block_input, before, after, taps)
    part = part / math.sqrt(rows_here * lat * lons_here * lon)

    left, right = part[:, : channels // 2], part[:, channels // 2 :]
    mine, other = jnp.where(core == 0, left, right), jnp.where(core == 0, right, left)
    mine = mine + lax.ppermute(other, "core", swap)
    mine = mine.reshape(2, 2, 2, 2, 2, -1, mine.shape[1])
    mine = halve(halve(mine, "y", 1, 1), "y", 2, 0)
    mine = halve(halve(mine, "z_lo", 1, 2), "z_lo", 2, 1)
    columns, mine = lax.optimization_barrier((columns, mine))
    chunk = halve(mine, "z_lo", 4, 0)
    high, width = chunk.shape

    fourier = unfold(columns, rows_here, orders_here, chans)
    degree = jnp.einsum("mla,mxa->mxl", leg_table, fourier, preferred_element_type=F32)
    degree = degree.reshape(orders_here, 2, chans, degrees)
    spec_grad = (degree * spec_filter.T).astype(BF16).transpose(3, 0, 1, 2)
    coeff = spec_coeff.transpose(1, 2, 3, 0).astype(F32)
    filter_part = jnp.sum(coeff * degree, axis=(0, 1)) / math.sqrt(2 * orders)

    pieces = degrees // width
    both = [chunk] + [filter_part[:, i * width : (i + 1) * width] for i in range(pieces)]
    both = to_all(jnp.concatenate(both, axis=0), ("x", "core"))
    cores = jnp.sum(both.reshape(-1, 2, *both.shape[1:]), axis=0)
    chunk = jnp.where(core == 0, cores[0, :high], cores[1, :high])
    both = jnp.concatenate([chunk, cores[0, high:] + cores[1, high:]], axis=0)
    both, edges = lax.optimization_barrier((both, (grad_rows[:, -1], grad_rows[:, 0])))
    edges = (
        lax.ppermute(edges[0], LON, ring(lon, 1)),
        lax.ppermute(edges[1], LON, ring(lon, -1)),
    )
    both = to_all(both, "z_hi")
    both, (before, after) = lax.optimization_barrier((both, edges))
    both = jnp.sum(both, axis=0)
    filter_grad = both[high:].reshape(pieces, chans, width).transpose(0, 2, 1)
    filter_grad = filter_grad.reshape(degrees, chans)

    input_grad = input_part(grad_rows, before, after, taps, tap_weight)

    mine = to_all(both[:high].astype(BF16), "z_lo").reshape(-1, width)
    mine = to_all(mine, ("core", "y")).reshape(2, -1, width)
    taps_grad = jnp.concatenate([mine[0], mine[1]], axis=1).astype(F32)
    taps_grad = taps_grad.reshape(len(taps), channels, channels)
    return (spec_grad, filter_grad, input_grad, taps_grad)


def solution(mesh):
    sizes = tuple(size for _, size in PARTS)
    names, sizes = zip(*PARTS)
    split = jax.sharding.Mesh(mesh.devices.reshape(sizes), names)
    in_specs = (
        P(LAT, LON, None),
        P(LAT, LON, None),
        P(LAT, None, None),
        P(None, LAT, None, LON),
        P(None, LON),
        P(),
        P(),
        P(),
    )
    out_specs = (P(None, LAT, None, LON), P(None, LON), P(LAT, LON, None), P())
    return jax.shard_map(
        on_device, mesh=split, in_specs=in_specs, out_specs=out_specs, check_vma=False
    )
```

```python
import functools
import math

import jax
import jax.numpy as jnp
import ml_dtypes
import numpy as np
from jax import lax
from jax.experimental import pallas as pl
from jax.experimental.pallas import tpu as pltpu
from jax.sharding import PartitionSpec as P

F32 = jnp.float32
BF16 = jnp.bfloat16
ROW = 8
LANES = 128


def ceil_to(value, step):
    return -(-value // step) * step


PARTS = (("x", 4), ("z_hi", 4), ("core", 2), ("y", 4), ("z_lo", 8))
LAT = ("x", "z_hi", "core")
LON = ("y", "z_lo")


def ring(size, step):
    return [(i, (i + step) % size) for i in range(size)]


def to_all(value, axes):
    count = lax.axis_size(axes)
    return lax.all_to_all(jnp.broadcast_to(value, (count, *value.shape)), axes, 0, 0)


def pairs(size, bit):
    return [(i, i ^ bit) for i in range(size)]


def halve(value, axis, bit, where):
    low = lax.index_in_dim(value, 0, where, keepdims=False)
    high = lax.index_in_dim(value, 1, where, keepdims=False)
    upper = (lax.axis_index(axis) & bit) != 0
    value, sent = jnp.where(upper, high, low), jnp.where(upper, low, high)
    received = lax.ppermute(sent.astype(BF16), axis, pairs(lax.axis_size(axis), bit))
    return value + received.astype(F32)


def transform_constants(sectors, sector, orders, chans):
    lon_total = sectors * sector
    width = ceil_to(sector, 16)
    turns = orders // sectors
    p, j, q, t = (np.arange(n) for n in (sectors, sectors, sector, turns))
    across = 2 * np.pi * (p[:, None] * j[None, :] % sectors) / sectors
    eye = np.eye(chans)
    across = np.concatenate([np.kron(np.cos(across), eye), np.kron(np.sin(across), eye)])
    phase = 2 * np.pi * (p[:, None] * q[None, :]) / lon_total
    twiddle = np.zeros((2, sectors, ROW, width))
    twiddle[0, :, :, :sector] = (np.cos(phase) / math.sqrt(lon_total))[:, None]
    twiddle[1, :, :, :sector] = (np.sin(phase) / math.sqrt(lon_total))[:, None]
    twiddle = np.repeat(twiddle.reshape(2, sectors, ROW * width), chans, axis=1)
    within = 2 * np.pi * (t[:, None] * q[None, :] % sector) / sector
    c, s = np.cos(within), np.sin(within)
    inner = np.zeros((turns, 2, ROW, 2, ROW, width))
    for row in range(ROW):
        inner[:, 0, row, 0, row, :sector] = c
        inner[:, 0, row, 1, row, :sector] = -s
        inner[:, 1, row, 0, row, :sector] = s
        inner[:, 1, row, 1, row, :sector] = c
    inner = inner.reshape(turns * 2 * ROW, 2 * ROW * width)
    kind = ml_dtypes.bfloat16
    return across.astype(kind), twiddle.astype(np.float32), inner.astype(kind)


def turn_kernel(x_ref, o_ref, s_ref):
    rows, lons, _ = x_ref.shape
    s_ref[...] = jnp.zeros_like(s_ref)
    s_ref[:rows, :lons, :] = x_ref[...]
    o_ref[...] = s_ref[...].reshape(-1, s_ref.shape[2]).T


def channels_first(field):
    rows, lons, channels = field.shape
    tall, wide = ceil_to(rows, ROW), ceil_to(lons, 16)
    return pl.pallas_call(
        turn_kernel,
        out_shape=jax.ShapeDtypeStruct((channels, tall * wide), field.dtype),
        scratch_shapes=[pltpu.VMEM((tall, wide, channels), field.dtype)],
        compiler_params=pltpu.CompilerParams(vmem_limit_bytes=32 << 20),
        cost_estimate=pl.CostEstimate(
            flops=0, transcendentals=0, bytes_accessed=4 * channels * tall * wide
        ),
        name="channels_first",
    )(field)


def fourier_kernel(blocks, turns, span, keep, r_ref, d_ref, tw_ref, w_ref, o_ref, g_ref):
    half = r_ref.shape[0]
    wide = tw_ref.shape[2]
    tall = blocks * ROW
    for block in range(blocks):
        field = r_ref[:, block * wide : (block + 1) * wide]
        a = jnp.dot(d_ref[:half], field, preferred_element_type=F32)
        b = jnp.dot(d_ref[half:], field, preferred_element_type=F32)
        re = (a * tw_ref[0] - b * tw_ref[1]).astype(BF16)
        im = (a * tw_ref[1] + b * tw_ref[0]).astype(BF16)
        nt = (((1,), (1,)), ((), ()))
        out = lax.dot_general(w_ref[:, :wide], re, nt, preferred_element_type=F32)
        out += lax.dot_general(w_ref[:, wide:], im, nt, preferred_element_type=F32)
        for t in range(turns):
            for r in range(2):
                g_ref[
                    r * tall + block * ROW : r * tall + (block + 1) * ROW,
                    t * half : (t + 1) * half,
                ] = out[(t * 2 + r) * ROW : (t * 2 + r + 1) * ROW]
    count = o_ref.shape[0]
    group = math.lcm(span, LANES)
    lane = lax.broadcasted_iota(jnp.int32, (keep, LANES), 1)
    rest = LANES - span
    for start in range(0, count * span, group):
        values = g_ref[:, start : start + group]
        for k in range(group // span):
            shift = (group - k * span) % group
            piece = pltpu.roll(values, shift, 1) if shift else values
            piece = piece[:, :LANES]
            tail = piece[keep:]
            folds = [pltpu.roll(tail, span - n * rest, 1) for n in range(span // rest)]
            folds.append(jnp.zeros((keep - len(folds) * tail.shape[0], LANES), F32))
            folded = jnp.concatenate(folds, axis=0)
            o_ref[start // span + k] = jnp.where(lane < span, piece[:keep], folded).astype(BF16)


def fold_sizes(rows, span):
    tall = 2 * ceil_to(rows, ROW)
    return tall, tall - ROW


def fourier_chunks(received, rows, sector, orders, groups):
    sectors, chans, lanes = received.shape
    blocks = ceil_to(rows, ROW) // ROW
    turns = orders // sectors
    span = orders // groups * chans
    tall, keep = fold_sizes(rows, span)
    across, twiddle, inner = transform_constants(sectors, sector, orders, chans)
    return pl.pallas_call(
        functools.partial(fourier_kernel, blocks, turns, span, keep),
        out_shape=jax.ShapeDtypeStruct((groups, keep, LANES), BF16),
        scratch_shapes=[pltpu.VMEM((tall, orders * chans), F32)],
        compiler_params=pltpu.CompilerParams(vmem_limit_bytes=48 << 20),
        cost_estimate=pl.CostEstimate(
            flops=2 * sectors * chans * lanes * (2 * sectors * chans + 2 * turns * ROW * 2),
            transcendentals=0,
            bytes_accessed=2 * received.size + 2 * groups * keep * LANES + 4 * twiddle.size,
        ),
        name="fourier_chunks",
    )(
        received.reshape(sectors * chans, lanes),
        jnp.asarray(across),
        jnp.asarray(twiddle),
        jnp.asarray(inner),
    )


def unfold_kernel(rows, span, q_ref, o_ref, s_ref):
    count, keep, _ = q_ref.shape
    tall = ceil_to(rows, ROW)
    rest = LANES - span
    lane = lax.broadcasted_iota(jnp.int32, (ROW, LANES), 1)
    used = count * rows
    if s_ref.shape[0] > used:
        s_ref[used:, :] = jnp.zeros((s_ref.shape[0] - used, s_ref.shape[1]), F32)
    for n in range(count):
        block = q_ref[n].astype(F32)
        tail = pltpu.roll(block[:ROW], rest, 1)
        for k in range(1, span // rest):
            piece = pltpu.roll(block[k * ROW : (k + 1) * ROW], (k + 1) * rest, 1)
            tail = jnp.where(lane < k * rest, tail, piece)
        s_ref[n * rows : (n + 1) * rows, :LANES] = block[:rows]
        middle = keep - tall
        s_ref[n * rows : n * rows + middle, LANES:] = block[tall:keep]
        s_ref[n * rows + middle : (n + 1) * rows, LANES:] = tail[: rows - middle]
    orders, both, _ = o_ref.shape
    chans = both // 2
    for r in range(2):
        flipped = s_ref[:, r * LANES : (r + 1) * LANES].T[:, :used].astype(BF16)
        for m in range(orders):
            o_ref[m, r * chans : (r + 1) * chans, :] = flipped[m * chans : (m + 1) * chans]


def unfold(received, rows, orders, chans):
    count = received.shape[0]
    used = count * rows
    return pl.pallas_call(
        functools.partial(unfold_kernel, rows, orders * chans),
        out_shape=jax.ShapeDtypeStruct((orders, 2 * chans, used), BF16),
        scratch_shapes=[pltpu.VMEM((ceil_to(used, LANES), 2 * LANES), F32)],
        compiler_params=pltpu.CompilerParams(vmem_limit_bytes=32 << 20),
        cost_estimate=pl.CostEstimate(
            flops=0, transcendentals=0, bytes_accessed=2 * received.size + 4 * orders * chans * used
        ),
        name="unfold",
    )(received)


def select(shifts, windows):
    picked = jnp.zeros_like(windows[0])
    for shift, window in zip((-1, 0, 1), windows):
        picked = jnp.where((shifts == shift)[:, None, None], window, picked)
    return picked


def tap_rows(cycle_weight, cycle_shift, rows):
    start = lax.axis_index(LAT) * rows
    weights = jnp.pad(cycle_weight, ((1, 1), (0, 0)))
    shifts = jnp.pad(cycle_shift, ((1, 1), (0, 0)))
    taps = []
    for index, offset in enumerate((-1, 0, 1)):
        weight = lax.dynamic_slice_in_dim(weights, start + 1 - offset, rows, 0)[:, index]
        shift = lax.dynamic_slice_in_dim(shifts, start + 1 - offset, rows, 0)[:, index]
        taps.append((1 - offset, weight, shift))
    return taps


def scaled(weight, field):
    return (weight[:, None, None] * field.astype(F32)).astype(BF16)


def taps_part(grad_rows, block_input, before, after, taps):
    rows, lons, channels = block_input.shape
    wide = jnp.concatenate([before[:, None], block_input, after[:, None]], axis=1)
    partials = []
    for first, weight, shift in taps:
        spread = scaled(weight, grad_rows[first : first + rows])
        picked = select(shift, [wide[:, 1 + k : 1 + k + lons] for k in (-1, 0, 1)])
        partials.append(
            lax.dot_general(
                picked.reshape(-1, channels),
                spread.reshape(-1, channels),
                (((0,), (0,)), ((), ())),
                preferred_element_type=F32,
            )
        )
    return jnp.concatenate(partials, axis=0)


def input_part(wide, taps, tap_weight):
    rows, lons, channels = wide.shape
    rows, lons = rows - 2, lons - 2
    total = jnp.zeros((rows * lons, channels), F32)
    for index, (first, weight, shift) in enumerate(taps):
        source = wide[first : first + rows]
        picked = select(shift, [source[:, 1 - k : 1 - k + lons] for k in (-1, 0, 1)])
        total = total + lax.dot_general(
            scaled(weight, picked).reshape(-1, channels),
            tap_weight[index],
            (((1,), (1,)), ((), ())),
            preferred_element_type=F32,
        )
    return total.reshape(rows, lons, channels).astype(BF16)


def on_device(
    grad_out, block_input, leg_table, spec_coeff, spec_filter, cycle_weight, cycle_shift, tap_weight
):
    rows_here, lons_here, channels = grad_out.shape
    lat, lon = lax.axis_size(LAT), lax.axis_size(LON)
    chans = channels // lon
    orders_here, degrees, _ = leg_table.shape
    orders = orders_here * lat
    core = lax.axis_index("core")
    swap = ring(2, 1)

    sent = channels_first(grad_out).reshape(lon, chans, -1)
    rows = lax.all_to_all(sent, LON, 0, 0)

    column = [jnp.concatenate([block_input[:, i], grad_out[:, i]], axis=0) for i in (0, -1)]
    before = lax.ppermute(column[1], LON, ring(lon, 1))
    after = lax.ppermute(column[0], LON, ring(lon, -1))
    before, after = before.reshape(2, rows_here, channels), after.reshape(2, rows_here, channels)
    wide = jnp.concatenate([before[1][:, None], grad_out, after[1][:, None]], axis=1)
    halos = (
        lax.ppermute(wide[-1], LAT, ring(lat, 1)),
        lax.ppermute(wide[0], LAT, ring(lat, -1)),
    )
    blocks = fourier_chunks(rows, rows_here, lons_here, orders, lat)
    blocks, (above, below) = lax.optimization_barrier((blocks, halos))
    columns = lax.all_to_all(blocks, LAT, 0, 0)

    wide = jnp.concatenate([above[None], wide, below[None]], axis=0)
    taps = tap_rows(cycle_weight, cycle_shift, rows_here)
    part = taps_part(wide[:, 1:-1], block_input, before[0], after[0], taps)
    part = part / math.sqrt(rows_here * lat * lons_here * lon)

    left, right = part[:, : channels // 2], part[:, channels // 2 :]
    mine, other = jnp.where(core == 0, left, right), jnp.where(core == 0, right, left)
    mine = mine + lax.ppermute(other, "core", swap)
    mine = mine.reshape(2, 2, 2, 2, 2, -1, mine.shape[1])
    mine = halve(halve(mine, "y", 1, 1), "y", 2, 0)
    mine = halve(halve(mine, "z_lo", 1, 2), "z_lo", 2, 1)
    chunk = halve(mine, "z_lo", 4, 0)
    high, width = chunk.shape

    fourier = unfold(columns, rows_here, orders_here, chans)
    degree = jnp.einsum("mla,mxa->mxl", leg_table, fourier, preferred_element_type=F32)
    degree = degree.reshape(orders_here, 2, chans, degrees)
    spec_grad = (degree * spec_filter.T).astype(BF16).transpose(3, 0, 1, 2)
    coeff = spec_coeff.transpose(1, 2, 3, 0).astype(F32)
    filter_part = jnp.sum(coeff * degree, axis=(0, 1)) / math.sqrt(2 * orders)

    pieces = degrees // width
    both = [chunk] + [filter_part[:, i * width : (i + 1) * width] for i in range(pieces)]
    both = to_all(jnp.concatenate(both, axis=0), ("x", "core"))
    cores = jnp.sum(both.reshape(-1, 2, *both.shape[1:]), axis=0)
    chunk = jnp.where(core == 0, cores[0, :high], cores[1, :high])
    both = jnp.concatenate([chunk, cores[0, high:] + cores[1, high:]], axis=0)
    both = jnp.sum(to_all(both, "z_hi"), axis=0)
    filter_grad = both[high:].reshape(pieces, chans, width).transpose(0, 2, 1)
    filter_grad = filter_grad.reshape(degrees, chans)

    input_grad = input_part(wide, taps, tap_weight)

    mine = to_all(both[:high].astype(BF16), "z_lo").reshape(-1, width)
    mine = to_all(mine, ("core", "y")).reshape(2, -1, width)
    taps_grad = jnp.concatenate([mine[0], mine[1]], axis=1).astype(F32)
    taps_grad = taps_grad.reshape(len(taps), channels, channels)
    return (spec_grad, filter_grad, input_grad, taps_grad)


def solution(mesh):
    sizes = tuple(size for _, size in PARTS)
    names, sizes = zip(*PARTS)
    split = jax.sharding.Mesh(mesh.devices.reshape(sizes), names)
    in_specs = (
        P(LAT, LON, None),
        P(LAT, LON, None),
        P(LAT, None, None),
        P(None, LAT, None, LON),
        P(None, LON),
        P(),
        P(),
        P(),
    )
    out_specs = (P(None, LAT, None, LON), P(None, LON), P(LAT, LON, None), P())
    return jax.shard_map(
        on_device, mesh=split, in_specs=in_specs, out_specs=out_specs, check_vma=False
    )
```

```python
import functools
import math

import jax
import jax.numpy as jnp
import ml_dtypes
import numpy as np
from jax import lax
from jax.experimental import pallas as pl
from jax.experimental.pallas import tpu as pltpu
from jax.sharding import PartitionSpec as P

F32 = jnp.float32
BF16 = jnp.bfloat16
ROW = 8
LANES = 128


def ceil_to(value, step):
    return -(-value // step) * step


PARTS = (("x", 4), ("z_hi", 4), ("core", 2), ("y", 4), ("z_lo", 8))
LAT = ("x", "z_hi", "core")
LON = ("y", "z_lo")


def ring(size, step):
    return [(i, (i + step) % size) for i in range(size)]


def to_all(value, axes):
    count = lax.axis_size(axes)
    return lax.all_to_all(jnp.broadcast_to(value, (count, *value.shape)), axes, 0, 0)


def pairs(size, bit):
    return [(i, i ^ bit) for i in range(size)]


def halve(value, axis, bit, where):
    low = lax.index_in_dim(value, 0, where, keepdims=False)
    high = lax.index_in_dim(value, 1, where, keepdims=False)
    upper = (lax.axis_index(axis) & bit) != 0
    value, sent = jnp.where(upper, high, low), jnp.where(upper, low, high)
    received = lax.ppermute(sent.astype(BF16), axis, pairs(lax.axis_size(axis), bit))
    return value + received.astype(F32)


def transform_constants(sectors, sector, orders, chans):
    lon_total = sectors * sector
    width = ceil_to(sector, 16)
    turns = orders // sectors
    p, j, q, t = (np.arange(n) for n in (sectors, sectors, sector, turns))
    across = 2 * np.pi * (p[:, None] * j[None, :] % sectors) / sectors
    eye = np.eye(chans)
    across = np.concatenate([np.kron(np.cos(across), eye), np.kron(np.sin(across), eye)])
    phase = 2 * np.pi * (p[:, None] * q[None, :]) / lon_total
    twiddle = np.zeros((2, sectors, ROW, width))
    twiddle[0, :, :, :sector] = (np.cos(phase) / math.sqrt(lon_total))[:, None]
    twiddle[1, :, :, :sector] = (np.sin(phase) / math.sqrt(lon_total))[:, None]
    twiddle = np.repeat(twiddle.reshape(2, sectors, ROW * width), chans, axis=1)
    within = 2 * np.pi * (t[:, None] * q[None, :] % sector) / sector
    c, s = np.cos(within), np.sin(within)
    inner = np.zeros((turns, 2, ROW, 2, ROW, width))
    for row in range(ROW):
        inner[:, 0, row, 0, row, :sector] = c
        inner[:, 0, row, 1, row, :sector] = -s
        inner[:, 1, row, 0, row, :sector] = s
        inner[:, 1, row, 1, row, :sector] = c
    inner = inner.reshape(turns * 2 * ROW, 2 * ROW * width)
    kind = ml_dtypes.bfloat16
    return across.astype(kind), twiddle.astype(np.float32), inner.astype(kind)


def turn_kernel(x_ref, o_ref, s_ref):
    rows, lons, _ = x_ref.shape
    s_ref[...] = jnp.zeros_like(s_ref)
    s_ref[:rows, :lons, :] = x_ref[...]
    o_ref[...] = s_ref[...].reshape(-1, s_ref.shape[2]).T


def channels_first(field):
    rows, lons, channels = field.shape
    tall, wide = ceil_to(rows, ROW), ceil_to(lons, 16)
    return pl.pallas_call(
        turn_kernel,
        out_shape=jax.ShapeDtypeStruct((channels, tall * wide), field.dtype),
        scratch_shapes=[pltpu.VMEM((tall, wide, channels), field.dtype)],
        compiler_params=pltpu.CompilerParams(vmem_limit_bytes=32 << 20),
        cost_estimate=pl.CostEstimate(
            flops=0, transcendentals=0, bytes_accessed=4 * channels * tall * wide
        ),
        name="channels_first",
    )(field)


def fourier_kernel(blocks, turns, span, keep, r_ref, d_ref, tw_ref, w_ref, o_ref, g_ref):
    half = r_ref.shape[0]
    wide = tw_ref.shape[2]
    tall = blocks * ROW
    for block in range(blocks):
        field = r_ref[:, block * wide : (block + 1) * wide]
        a = jnp.dot(d_ref[:half], field, preferred_element_type=F32)
        b = jnp.dot(d_ref[half:], field, preferred_element_type=F32)
        re = (a * tw_ref[0] - b * tw_ref[1]).astype(BF16)
        im = (a * tw_ref[1] + b * tw_ref[0]).astype(BF16)
        nt = (((1,), (1,)), ((), ()))
        out = lax.dot_general(w_ref[:, :wide], re, nt, preferred_element_type=F32)
        out += lax.dot_general(w_ref[:, wide:], im, nt, preferred_element_type=F32)
        for t in range(turns):
            for r in range(2):
                g_ref[
                    r * tall + block * ROW : r * tall + (block + 1) * ROW,
                    t * half : (t + 1) * half,
                ] = out[(t * 2 + r) * ROW : (t * 2 + r + 1) * ROW]
    count = o_ref.shape[0]
    group = math.lcm(span, LANES)
    lane = lax.broadcasted_iota(jnp.int32, (keep, LANES), 1)
    rest = LANES - span
    for start in range(0, count * span, group):
        values = g_ref[:, start : start + group]
        for k in range(group // span):
            shift = (group - k * span) % group
            piece = pltpu.roll(values, shift, 1) if shift else values
            piece = piece[:, :LANES]
            tail = piece[keep:]
            folds = [pltpu.roll(tail, span - n * rest, 1) for n in range(span // rest)]
            folds.append(jnp.zeros((keep - len(folds) * tail.shape[0], LANES), F32))
            folded = jnp.concatenate(folds, axis=0)
            o_ref[start // span + k] = jnp.where(lane < span, piece[:keep], folded).astype(BF16)


def fold_sizes(rows, span):
    tall = 2 * ceil_to(rows, ROW)
    return tall, tall - ROW


def fourier_chunks(received, rows, sector, orders, groups):
    sectors, chans, lanes = received.shape
    blocks = ceil_to(rows, ROW) // ROW
    turns = orders // sectors
    span = orders // groups * chans
    tall, keep = fold_sizes(rows, span)
    across, twiddle, inner = transform_constants(sectors, sector, orders, chans)
    return pl.pallas_call(
        functools.partial(fourier_kernel, blocks, turns, span, keep),
        out_shape=jax.ShapeDtypeStruct((groups, keep, LANES), BF16),
        scratch_shapes=[pltpu.VMEM((tall, orders * chans), F32)],
        compiler_params=pltpu.CompilerParams(vmem_limit_bytes=48 << 20),
        cost_estimate=pl.CostEstimate(
            flops=2 * sectors * chans * lanes * (2 * sectors * chans + 2 * turns * ROW * 2),
            transcendentals=0,
            bytes_accessed=2 * received.size + 2 * groups * keep * LANES + 4 * twiddle.size,
        ),
        name="fourier_chunks",
    )(
        received.reshape(sectors * chans, lanes),
        jnp.asarray(across),
        jnp.asarray(twiddle),
        jnp.asarray(inner),
    )


def unfold_kernel(rows, span, q_ref, o_ref, s_ref):
    count, keep, _ = q_ref.shape
    tall = ceil_to(rows, ROW)
    rest = LANES - span
    lane = lax.broadcasted_iota(jnp.int32, (ROW, LANES), 1)
    used = count * rows
    if s_ref.shape[0] > used:
        s_ref[used:, :] = jnp.zeros((s_ref.shape[0] - used, s_ref.shape[1]), F32)
    for n in range(count):
        block = q_ref[n].astype(F32)
        tail = pltpu.roll(block[:ROW], rest, 1)
        for k in range(1, span // rest):
            piece = pltpu.roll(block[k * ROW : (k + 1) * ROW], (k + 1) * rest, 1)
            tail = jnp.where(lane < k * rest, tail, piece)
        s_ref[n * rows : (n + 1) * rows, :LANES] = block[:rows]
        middle = keep - tall
        s_ref[n * rows : n * rows + middle, LANES:] = block[tall:keep]
        s_ref[n * rows + middle : (n + 1) * rows, LANES:] = tail[: rows - middle]
    orders, both, _ = o_ref.shape
    chans = both // 2
    for r in range(2):
        flipped = s_ref[:, r * LANES : (r + 1) * LANES].T[:, :used].astype(BF16)
        for m in range(orders):
            o_ref[m, r * chans : (r + 1) * chans, :] = flipped[m * chans : (m + 1) * chans]


def unfold(received, rows, orders, chans):
    count = received.shape[0]
    used = count * rows
    return pl.pallas_call(
        functools.partial(unfold_kernel, rows, orders * chans),
        out_shape=jax.ShapeDtypeStruct((orders, 2 * chans, used), BF16),
        scratch_shapes=[pltpu.VMEM((ceil_to(used, LANES), 2 * LANES), F32)],
        compiler_params=pltpu.CompilerParams(vmem_limit_bytes=32 << 20),
        cost_estimate=pl.CostEstimate(
            flops=0, transcendentals=0, bytes_accessed=2 * received.size + 4 * orders * chans * used
        ),
        name="unfold",
    )(received)


def select(shifts, windows):
    picked = jnp.zeros_like(windows[0])
    for shift, window in zip((-1, 0, 1), windows):
        picked = jnp.where((shifts == shift)[:, None, None], window, picked)
    return picked


def tap_rows(cycle_weight, cycle_shift, rows):
    start = lax.axis_index(LAT) * rows
    weights = jnp.pad(cycle_weight, ((1, 1), (0, 0)))
    shifts = jnp.pad(cycle_shift, ((1, 1), (0, 0)))
    taps = []
    for index, offset in enumerate((-1, 0, 1)):
        weight = lax.dynamic_slice_in_dim(weights, start + 1 - offset, rows, 0)[:, index]
        shift = lax.dynamic_slice_in_dim(shifts, start + 1 - offset, rows, 0)[:, index]
        taps.append((1 - offset, weight, shift))
    return taps


def scaled(weight, field):
    return (weight[:, None, None] * field.astype(F32)).astype(BF16)


def taps_part(grad_rows, block_input, before, after, taps):
    rows, lons, channels = block_input.shape
    wide = jnp.concatenate([before[:, None], block_input, after[:, None]], axis=1)
    partials = []
    for first, weight, shift in taps:
        spread = scaled(weight, grad_rows[first : first + rows])
        picked = select(shift, [wide[:, 1 + k : 1 + k + lons] for k in (-1, 0, 1)])
        partials.append(
            lax.dot_general(
                picked.reshape(-1, channels),
                spread.reshape(-1, channels),
                (((0,), (0,)), ((), ())),
                preferred_element_type=F32,
            )
        )
    return jnp.concatenate(partials, axis=0)


def input_part(grad_rows, before, after, taps, tap_weight):
    rows, lons, channels = grad_rows.shape
    rows -= 2
    wide = jnp.concatenate([before[:, None], grad_rows, after[:, None]], axis=1)
    total = jnp.zeros((rows * lons, channels), F32)
    for index, (first, weight, shift) in enumerate(taps):
        source = wide[first : first + rows]
        picked = select(shift, [source[:, 1 - k : 1 - k + lons] for k in (-1, 0, 1)])
        total = total + lax.dot_general(
            scaled(weight, picked).reshape(-1, channels),
            tap_weight[index],
            (((1,), (1,)), ((), ())),
            preferred_element_type=F32,
        )
    return total.reshape(rows, lons, channels).astype(BF16)


def on_device(
    grad_out, block_input, leg_table, spec_coeff, spec_filter, cycle_weight, cycle_shift, tap_weight
):
    rows_here, lons_here, channels = grad_out.shape
    lat, lon = lax.axis_size(LAT), lax.axis_size(LON)
    chans = channels // lon
    orders_here, degrees, _ = leg_table.shape
    orders = orders_here * lat
    core = lax.axis_index("core")
    swap = ring(2, 1)

    sent = channels_first(grad_out).reshape(lon, chans, -1)
    rows = lax.all_to_all(sent, LON, 0, 0)

    halos = (
        lax.ppermute(grad_out[-1], LAT, ring(lat, 1)),
        lax.ppermute(grad_out[0], LAT, ring(lat, -1)),
        lax.ppermute(block_input[:, -1], LON, ring(lon, 1)),
        lax.ppermute(block_input[:, 0], LON, ring(lon, -1)),
    )
    blocks = fourier_chunks(rows, rows_here, lons_here, orders, lat)
    blocks, (above, below, before, after) = lax.optimization_barrier((blocks, halos))
    columns = lax.all_to_all(blocks, LAT, 0, 0)

    grad_rows = jnp.concatenate([above[None], grad_out, below[None]], axis=0)
    taps = tap_rows(cycle_weight, cycle_shift, rows_here)
    part = taps_part(grad_rows, block_input, before, after, taps)
    part = part / math.sqrt(rows_here * lat * lons_here * lon)

    left, right = part[:, : channels // 2], part[:, channels // 2 :]
    mine, other = jnp.where(core == 0, left, right), jnp.where(core == 0, right, left)
    mine = mine + lax.ppermute(other, "core", swap)
    mine = mine.reshape(2, 2, 2, 2, 2, -1, mine.shape[1])
    mine = halve(halve(mine, "y", 1, 1), "y", 2, 0)
    mine = halve(halve(mine, "z_lo", 1, 2), "z_lo", 2, 1)
    chunk = halve(mine, "z_lo", 4, 0)
    high, width = chunk.shape

    fourier = unfold(columns, rows_here, orders_here, chans)
    degree = jnp.einsum("mla,mxa->mxl", leg_table, fourier, preferred_element_type=F32)
    degree = degree.reshape(orders_here, 2, chans, degrees)
    spec_grad = (degree * spec_filter.T).astype(BF16).transpose(3, 0, 1, 2)
    coeff = spec_coeff.transpose(1, 2, 3, 0).astype(F32)
    filter_part = jnp.sum(coeff * degree, axis=(0, 1)) / math.sqrt(2 * orders)

    pieces = degrees // width
    both = [chunk] + [filter_part[:, i * width : (i + 1) * width] for i in range(pieces)]
    both = to_all(jnp.concatenate(both, axis=0), ("x", "core"))
    cores = jnp.sum(both.reshape(-1, 2, *both.shape[1:]), axis=0)
    chunk = jnp.where(core == 0, cores[0, :high], cores[1, :high])
    both = jnp.concatenate([chunk, cores[0, high:] + cores[1, high:]], axis=0)
    both, edges = lax.optimization_barrier((both, (grad_rows[:, -1], grad_rows[:, 0])))
    edges = (
        lax.ppermute(edges[0], LON, ring(lon, 1)),
        lax.ppermute(edges[1], LON, ring(lon, -1)),
    )
    both = to_all(both, "z_hi")
    both, (before, after) = lax.optimization_barrier((both, edges))
    both = jnp.sum(both, axis=0)
    filter_grad = both[high:].reshape(pieces, chans, width).transpose(0, 2, 1)
    filter_grad = filter_grad.reshape(degrees, chans)

    input_grad = input_part(grad_rows, before, after, taps, tap_weight)

    mine = to_all(both[:high].astype(BF16), "z_lo").reshape(-1, width)
    mine = to_all(mine, ("core", "y")).reshape(2, -1, width)
    taps_grad = jnp.concatenate([mine[0], mine[1]], axis=1).astype(F32)
    taps_grad = taps_grad.reshape(len(taps), channels, channels)
    return (spec_grad, filter_grad, input_grad, taps_grad)


def solution(mesh):
    sizes = tuple(size for _, size in PARTS)
    names, sizes = zip(*PARTS)
    split = jax.sharding.Mesh(mesh.devices.reshape(sizes), names)
    in_specs = (
        P(LAT, LON, None),
        P(LAT, LON, None),
        P(LAT, None, None),
        P(None, LAT, None, LON),
        P(None, LON),
        P(),
        P(),
        P(),
    )
    out_specs = (P(None, LAT, None, LON), P(None, LON), P(LAT, LON, None), P())
    return jax.shard_map(
        on_device, mesh=split, in_specs=in_specs, out_specs=out_specs, check_vma=False
    )
```
